256 devices in a mesh: dp: 32 (over y, x, core), tensor: 8 (over z).
Axes of the slice: x: 4, y: 4, z: 8, core: 2. Of those that a mesh axis runs over, the one named last changes fastest.
Arguments:
- patches: bfloat16 [16384, 1280], P('dp'), may hold values from -6 to 6
- window_ids: int32 [32, 512], P('dp'), may hold values from 0 to 15, never falling along the last dimension, each value on 1 to 64 neighbouring positions
- vit_gain: float32 [1280], replicated, may hold values from 0.5 to 2
- qkv_weight: bfloat16 [3, 1280, 1280], P(None, None, 'tensor'), may hold values from -0.15625 to 0.15625
- out_weight: bfloat16 [1280, 1280], P('tensor'), may hold values from -0.15625 to 0.15625
- merge_gain: float32 [1280], replicated, may hold values from 0.5 to 2
- merger_weight: bfloat16 [5120, 3584], P(None, 'tensor'), may hold values from -0.078125 to 0.078125
- audio: bfloat16 [12288, 3584], P('dp', 'tensor'), may hold values from -6 to 6
- span_lengths: int32 [32, 32], replicated, may hold values from 8 to 32, as said below
- span_time: int32 [32, 32], replicated, may hold values from 0 to 31, each once within a row
- llm_gain: float32 [3584], replicated, may hold values from 0.5 to 2
- gate_weight: bfloat16 [3584, 9472], P('dp', 'tensor'), may hold values from -0.09375 to 0.09375
- up_weight: bfloat16 [3584, 9472], P('dp', 'tensor'), may hold values from -0.09375 to 0.09375
- down_weight: bfloat16 [9472, 3584], P('tensor', 'dp'), may hold values from -0.0625 to 0.0625
Outputs:
- mixed: bfloat16 [16384, 3584], P(('dp', 'tensor'))
The draws below stay inside these ranges and needn't reach their ends.
Inputs may be any that keep to these rules, and one draw needn't show every extreme that they name: `span_lengths`: every row and every column sums to 512; every row and every column holds the value 32 at least once. `span_time`: each row is a permutation of the owners' numbers. `window_ids`: window numbers never fall along a row; a window holds at most 64 patches.
All inputs are finite; a program needn't handle non-finite values.
Results may differ from the reference program's by a relative error of at most 0.017.
Values may be sent and summed in bfloat16 or wider, within the bound.
No kernel may reach another device: no remote copies, remote signals or barrier semaphores. Data moves between devices by JAX's collectives and lax.ppermute only.
A program may use at most 128 MiB of HBM per device.

```python
import math
import jax
import jax.numpy as jnp
import numpy as np
from jax import lax

D_VIT = 1280
VIT_HEADS = 16
HEAD_VIT = 80
WINDOW = 64
D = 3584
FFW = 9472
PATCH_GRP = 512
AUD_GRP = 384
SEQ_ROWS = 512
PATCHES = 16384
AUDIO = 12288
N_DP = 32
N_TENSOR = 8


def draw_span_lengths(key, part):
    order = jax.random.permutation(jax.random.fold_in(key, 17), N_DP).astype(jnp.int32)
    owners = jnp.arange(N_DP, dtype=jnp.int32)
    columns = jnp.arange(N_DP, dtype=jnp.int32)
    first = (columns[None, :] == order[owners][:, None]).astype(jnp.int32)
    second = (columns[None, :] == order[(owners + 1) % N_DP][:, None]).astype(jnp.int32)
    third = (columns[None, :] == order[(owners + 2) % N_DP][:, None]).astype(jnp.int32)
    base = SEQ_ROWS // N_DP
    half = base // 2
    return (base + half * (2 * first - second - third)).astype(jnp.int32)


def block_scale(key, shape, cuts, smallest, top_value):
    def one(dim, blocks):
        draws = jax.random.uniform(jax.random.fold_in(jax.random.fold_in(key, 6), dim), (blocks,), jnp.float32, smallest / len(cuts), top_value / len(cuts))
        return jnp.repeat(jnp.exp(draws), shape[dim] // blocks).reshape((-1,) + (1,) * (len(shape) - dim - 1))

    level = one(*cuts[0])
    for cut in cuts[1:]:
        level = level * one(*cut)
    return level


def profile(amount, total, bound, lean):
    portions = [(1 << 20) // math.isqrt(standing ** lean) + 1 for standing in range(2, amount + 1)]
    rest, counts = total - bound - (amount - 1), [1] * (amount - 1)
    while rest > 0:
        movable = [i for i in range(amount - 1) if counts[i] < bound]
        mass, left = sum([portions[i] for i in movable]), rest
        for i in movable:
            extra = min(bound - counts[i], max(1, left * portions[i] // mass), rest)
            counts[i] = counts[i] + extra
            rest = rest - extra
    return np.array([bound] + counts)


def uneven_parts(rng, number_of, total, reach, skew):
    if number_of == 2:
        one = jax.random.randint(rng, (), max(1, total - reach), min(reach, total - 1) + 1)
        return jnp.stack([one, total - one])
    lengths = jnp.asarray(profile(number_of, total, reach, skew), jnp.int32)
    pairs = (number_of - 1) // 2
    giver, sink = lengths[1:1 + 2 * pairs:2], lengths[2:2 + 2 * pairs:2]
    margin = jnp.minimum(giver - 1, reach - sink)
    shifted = jax.random.randint(jax.random.fold_in(rng, 1), (pairs,), 0, 1 << 20) % (margin + 1)
    lengths = lengths.at[1:1 + 2 * pairs:2].set(giver - shifted).at[2:2 + 2 * pairs:2].set(sink + shifted)
    return lengths[jax.random.permutation(jax.random.fold_in(rng, 2), number_of)]


def scatter_about(own_key, extent, deviation, most, shards=(), kind=jnp.bfloat16):
    drawn = jax.random.normal(own_key, extent, jnp.float32) * deviation
    if len(shards) > 0:
        drawn = block_scale(own_key, extent, shards, -0.22, 0.18) * drawn
    return jnp.clip(drawn, min=-most, max=most).astype(kind)


def setup_inputs(seed: int = 0) -> dict:
    key_list = jax.random.split(jax.random.key(seed), 15)
    return {
        "patches": scatter_about(key_list[0], (PATCHES, D_VIT), 1.0, 6.0, ((0, 32),)),
        "window_ids": jax.vmap(lambda own: jnp.searchsorted(jnp.cumsum(uneven_parts(own, 2 * PATCH_GRP // WINDOW, PATCH_GRP, WINDOW, 1)), jnp.arange(PATCH_GRP), side="right"))(jax.random.split(key_list[1], N_DP)).reshape((N_DP, PATCH_GRP)).astype(jnp.int32),
        "vit_gain": jnp.clip(jnp.exp(jax.random.uniform(key_list[2], (D_VIT,), jnp.float32, math.log(0.5), math.log(2.0))), 0.5, 2.0),
        "qkv_weight": scatter_about(key_list[3], (3, D_VIT, D_VIT), D_VIT ** -0.5, 0.15625, ((2, 8),)),
        "out_weight": scatter_about(key_list[4], (D_VIT, D_VIT), D_VIT ** -0.5, 0.15625, ((0, 8),)),
        "merge_gain": jnp.clip(jnp.exp(jax.random.uniform(key_list[5], (D_VIT,), jnp.float32, math.log(0.5), math.log(2.0))), 0.5, 2.0),
        "merger_weight": scatter_about(key_list[6], (4 * D_VIT, D), (4 * D_VIT) ** -0.5, 0.078125, ((1, 8),)),
        "audio": scatter_about(key_list[7], (AUDIO, D), 1.0, 6.0, ((0, 32), (1, 8))),
        "span_lengths": draw_span_lengths(jax.random.fold_in(key_list[14], 71), 0),
        "span_time": jax.vmap(lambda own: jax.random.permutation(own, N_DP))(jax.random.split(key_list[9], N_DP)).reshape((N_DP, N_DP)).astype(jnp.int32),
        "llm_gain": jnp.clip(jnp.exp(jax.random.uniform(key_list[10], (D,), jnp.float32, math.log(0.5), math.log(2.0))), 0.5, 2.0),
        "gate_weight": scatter_about(key_list[11], (D, FFW), D ** -0.5, 0.09375, ((0, 32), (1, 8))),
        "up_weight": scatter_about(key_list[12], (D, FFW), D ** -0.5, 0.09375, ((0, 32), (1, 8))),
        "down_weight": scatter_about(key_list[13], (FFW, D), FFW ** -0.5, 0.0625, ((0, 8), (1, 32))),
    }


EPSILON = 1e-06

def rms_scale(values, gain):
    wide = values.astype(jnp.float32)
    meansq = lax.optimization_barrier(jnp.mean(wide * wide, axis=-1, keepdims=True))
    return wide * lax.rsqrt(meansq + EPSILON) * gain.astype(jnp.float32)

def vit_owner(frames, windows, vit_gain, qkv_weight, out_weight, merge_gain, merger_weight):
    patch_count = frames.shape[0]
    normed = rms_scale(frames, vit_gain).astype(jnp.bfloat16)
    query = jnp.dot(normed, qkv_weight[0], preferred_element_type=jnp.float32).astype(jnp.bfloat16)
    keys = jnp.dot(normed, qkv_weight[1], preferred_element_type=jnp.float32).astype(jnp.bfloat16)
    values = jnp.dot(normed, qkv_weight[2], preferred_element_type=jnp.float32).astype(jnp.bfloat16)
    query = query.reshape(patch_count, VIT_HEADS, HEAD_VIT).astype(jnp.float32)
    keys = keys.reshape(patch_count, VIT_HEADS, HEAD_VIT).astype(jnp.float32)
    values = values.reshape(patch_count, VIT_HEADS, HEAD_VIT).astype(jnp.float32)
    scores = jnp.einsum('phe,qhe->hpq', query, keys) / math.sqrt(HEAD_VIT)
    same = windows[:, None] == windows[None, :]
    scores = jnp.where(same[None], scores, -1e+30)
    probs = jax.nn.softmax(scores, axis=-1).astype(jnp.bfloat16)
    context = jnp.einsum('hpq,qhe->phe', probs.astype(jnp.float32), values).astype(jnp.bfloat16)
    grouped = context.reshape(patch_count, N_TENSOR, D_VIT // N_TENSOR).astype(jnp.float32)
    out_grouped = out_weight.reshape(N_TENSOR, D_VIT // N_TENSOR, D_VIT).astype(jnp.float32)
    partial_value = jnp.einsum('pge,ged->gpd', grouped, out_grouped).astype(jnp.bfloat16)
    attended = lax.optimization_barrier(jnp.sum(partial_value.astype(jnp.float32), axis=0))
    encoded = (frames.astype(jnp.float32) + attended).astype(jnp.bfloat16)
    merged = rms_scale(encoded, merge_gain).astype(jnp.bfloat16).reshape(patch_count // 4, 4 * D_VIT)
    return jnp.dot(merged, merger_weight, preferred_element_type=jnp.float32).astype(jnp.bfloat16)

def alternate(video, audio, span_lengths, span_time):
    source = jnp.concatenate([video, audio.reshape(N_DP, AUD_GRP, D)], axis=1)
    flat = source.reshape(N_DP * SEQ_ROWS, D)
    starts = jnp.cumsum(span_lengths, axis=1).astype(jnp.int32) - span_lengths
    arrival = span_time.T
    earlier = arrival[:, None, :] < arrival[None, :, :]
    offsets = lax.optimization_barrier(jnp.sum(jnp.where(earlier, span_lengths[:, None, :], 0), axis=0)).astype(jnp.int32)
    position = jnp.arange(SEQ_ROWS, dtype=jnp.int32)
    lower = offsets[:, :, None]
    inside = (position[None, None, :] >= lower) & (position[None, None, :] < lower + span_lengths[:, :, None])
    owners = jnp.arange(N_DP, dtype=jnp.int32)[:, None, None]
    source_row = owners * SEQ_ROWS + starts[:, :, None] + position[None, None, :] - lower
    picked = lax.optimization_barrier(jnp.sum(jnp.where(inside, source_row, 0), axis=0)).astype(jnp.int32)
    return jnp.take(flat, picked.reshape(-1), axis=0).reshape(N_DP, SEQ_ROWS, D)

def llm_owner(sequence, llm_gain, gate_weight, up_weight, down_weight):
    normed = rms_scale(sequence, llm_gain).astype(jnp.bfloat16)
    gate = jnp.dot(normed, gate_weight, preferred_element_type=jnp.float32)
    upward = jnp.dot(normed, up_weight, preferred_element_type=jnp.float32)
    hidden = (jax.nn.silu(gate) * upward).astype(jnp.bfloat16)
    width = FFW // N_TENSOR
    total = jnp.zeros((sequence.shape[0], D), jnp.float32)
    for group in range(N_TENSOR):
        piece = jnp.dot(hidden[:, group * width:(group + 1) * width], down_weight[group * width:(group + 1) * width], preferred_element_type=jnp.float32).astype(jnp.bfloat16)
        total = total + piece.astype(jnp.float32)
    return (sequence.astype(jnp.float32) + total).astype(jnp.bfloat16)

def reference(patches, window_ids, vit_gain, qkv_weight, out_weight, merge_gain, merger_weight, audio, span_lengths, span_time, llm_gain, gate_weight, up_weight, down_weight):
    frames_all = patches.reshape(N_DP, PATCH_GRP, D_VIT)

    def one_owner(inputs):
        return vit_owner(inputs[0], inputs[1], vit_gain, qkv_weight, out_weight, merge_gain, merger_weight)
    video = lax.map(one_owner, (frames_all, window_ids))
    sequences = alternate(video, audio, span_lengths, span_time)

    def one_sequence(sequence):
        return llm_owner(sequence, llm_gain, gate_weight, up_weight, down_weight)
    mixed = lax.map(one_sequence, sequences)
    return mixed.reshape(N_DP * SEQ_ROWS, D)
```

```python
import math

import jax
import jax.numpy as jnp
from jax import lax
from jax.sharding import PartitionSpec as P

HEAD_VIT = 80
EPSILON = 1e-06


def rms_scale(values, gain):
    wide = values.astype(jnp.float32)
    meansq = jnp.mean(wide * wide, axis=-1, keepdims=True)
    return wide * lax.rsqrt(meansq + EPSILON) * gain


def ring_blocks(x, axis):
    n = lax.axis_size(axis)
    up = [(i, (i + 1) % n) for i in range(n)]
    down = [(i, (i - 1) % n) for i in range(n)]
    blocks = {0: x}
    a = b = x
    for k in range(1, n // 2 + 1):
        a = lax.ppermute(a, axis, up)
        blocks[-k] = a
        if k < n - n // 2:
            b = lax.ppermute(b, axis, down)
            blocks[k] = b
    return blocks


def body(
    patches,
    window_ids,
    vit_gain,
    qkv_weight,
    out_weight,
    merge_gain,
    merger_weight,
    audio,
    span_lengths,
    span_time,
    llm_gain,
    gate_weight,
    up_weight,
    down_weight,
):
    patch_count, d_vit = patches.shape
    n_tensor = lax.axis_size("tensor")
    owner_count = lax.axis_size("dp")
    owner = lax.axis_index("dp")
    plane = lax.axis_index("tensor")
    core = lax.rem(owner, 2)

    hidden_units = gate_weight.shape[1]
    stacked = jnp.concatenate([gate_weight, up_weight, down_weight.T], axis=1)
    whole = lax.all_gather(stacked, "dp", axis=0, tiled=True)

    own_head = lax.dynamic_slice_in_dim(out_weight, core * HEAD_VIT, HEAD_VIT, 0)
    got = ring_blocks(own_head, "tensor")
    order = sorted(got)
    mine = jnp.stack([got[k] for k in order])
    swap = [(i, i ^ 1) for i in range(owner_count)]
    other = lax.ppermute(mine, "dp", swap)
    out_full = jnp.concatenate([mine, other], axis=1).reshape(-1, d_vit)

    heads_here = qkv_weight.shape[2] // HEAD_VIT
    normed = rms_scale(patches, vit_gain).astype(jnp.bfloat16)
    query, keys, values = (
        jnp.dot(normed, qkv_weight[k], preferred_element_type=jnp.float32)
        .astype(jnp.bfloat16)
        .reshape(patch_count, heads_here, HEAD_VIT)
        for k in range(3)
    )
    scores = jnp.einsum(
        "phe,qhe->hpq", query, keys, preferred_element_type=jnp.float32
    ) / math.sqrt(HEAD_VIT)
    windows = window_ids[0]
    same = windows[:, None] == windows[None, :]
    scores = jnp.where(same[None], scores, -1e30)
    probs = jax.nn.softmax(scores, axis=-1).astype(jnp.bfloat16)
    context = jnp.einsum(
        "hpq,qhe->hpe", probs, values, preferred_element_type=jnp.float32
    ).astype(jnp.bfloat16)
    first, second = context[0], context[1]
    context = jnp.where(
        core == 0,
        jnp.concatenate([first, second], axis=1),
        jnp.concatenate([second, first], axis=1),
    )
    got = ring_blocks(context, "tensor")
    context_full = jnp.concatenate([got[k] for k in order], axis=1)
    attended = jnp.dot(context_full, out_full, preferred_element_type=jnp.float32)
    encoded = (patches.astype(jnp.float32) + attended).astype(jnp.bfloat16)
    merged = (
        rms_scale(encoded, merge_gain).astype(jnp.bfloat16).reshape(patch_count // 4, 4 * d_vit)
    )
    video = jnp.dot(merged, merger_weight, preferred_element_type=jnp.float32).astype(jnp.bfloat16)

    video_rows = video.shape[0]
    seq_count = video_rows + audio.shape[0]
    capacity = 2 * seq_count // owner_count
    sent_lengths = span_lengths[owner]
    starts = jnp.cumsum(sent_lengths) - sent_lengths
    slot_index = jnp.arange(capacity, dtype=jnp.int32)
    row_of_slot = jnp.where(
        slot_index[None, :] < sent_lengths[:, None], starts[:, None] + slot_index[None, :], -1
    ).reshape(-1)
    row = jnp.arange(seq_count, dtype=jnp.int32)
    select = (row_of_slot[:, None] == row[None, :]).astype(jnp.bfloat16)
    from_audio = jnp.dot(select[:, video_rows:], audio, preferred_element_type=jnp.float32)
    from_audio = lax.optimization_barrier(from_audio.astype(jnp.bfloat16))
    outgoing = (
        jnp.dot(select[:, :video_rows], video, preferred_element_type=jnp.float32)
        + from_audio.astype(jnp.float32)
    ).astype(jnp.bfloat16)
    incoming = lax.all_to_all(outgoing, "dp", split_axis=0, concat_axis=0, tiled=True)
    taken_lengths = span_lengths[:, owner]
    arrival = span_time[owner]
    earlier = arrival[:, None] < arrival[None, :]
    offsets = jnp.sum(jnp.where(earlier, taken_lengths[:, None], 0), axis=0)
    target = jnp.where(
        slot_index[None, :] < taken_lengths[:, None], offsets[:, None] + slot_index[None, :], -1
    ).reshape(-1)
    pick = (row[:, None] == target[None, :]).astype(jnp.bfloat16)
    sequence = jnp.dot(pick, incoming, preferred_element_type=jnp.float32).astype(jnp.bfloat16)

    got = ring_blocks(sequence, "tensor")
    buffer = jnp.zeros((n_tensor, *sequence.shape), sequence.dtype)
    for k in order:
        buffer = lax.dynamic_update_index_in_dim(
            buffer, got[k], lax.rem(plane + k + n_tensor, n_tensor), 0
        )
    features = jnp.moveaxis(buffer, 0, 1).reshape(seq_count, -1)
    normed_seq = rms_scale(features, llm_gain).astype(jnp.bfloat16)
    both = jnp.dot(
        normed_seq, whole[:, : 2 * hidden_units], preferred_element_type=jnp.float32
    )
    hidden = (jax.nn.silu(both[:, :hidden_units]) * both[:, hidden_units:]).astype(jnp.bfloat16)
    hidden = lax.optimization_barrier(hidden)
    terms = lax.dot_general(
        hidden,
        whole[:, 2 * hidden_units :],
        (((1,), (1,)), ((), ())),
        preferred_element_type=jnp.float32,
    )
    summed = lax.psum_scatter(
        terms.astype(jnp.bfloat16), "tensor", scatter_dimension=0, tiled=True
    ).astype(jnp.float32)
    own_count = summed.shape[0]
    own_rows = lax.dynamic_slice_in_dim(features, plane * own_count, own_count, 0)
    return (own_rows.astype(jnp.float32) + summed).astype(jnp.bfloat16)


def solution(mesh):
    return jax.shard_map(
        body,
        mesh=mesh,
        in_specs=(
            P("dp", None),
            P("dp", None),
            P(),
            P(None, None, "tensor"),
            P("tensor", None),
            P(),
            P(None, "tensor"),
            P("dp", "tensor"),
            P(),
            P(),
            P(),
            P("dp", "tensor"),
            P("dp", "tensor"),
            P("tensor", "dp"),
        ),
        out_specs=P(("dp", "tensor"), None),
        check_vma=False,
    )
```

```python
import functools
import math

import jax
import jax.numpy as jnp
from jax import lax
from jax.experimental import pallas as pl
from jax.experimental.pallas import tpu as pltpu
from jax.sharding import PartitionSpec as P

HEAD_VIT = 80
EPSILON = 1e-06
VMEM = pltpu.MemorySpace.VMEM
SMEM = pltpu.MemorySpace.SMEM
BF16 = jnp.bfloat16
F32 = jnp.float32


def ring_blocks(x, axis, beside=None, rounds_first=2):
    n = lax.axis_size(axis)
    up = [(i, (i + 1) % n) for i in range(n)]
    down = [(i, (i - 1) % n) for i in range(n)]
    blocks = {0: x}
    a = b = x
    for k in range(1, n // 2 + 1):
        a = lax.ppermute(a, axis, up)
        if k < n - n // 2:
            b = lax.ppermute(b, axis, down)
        if beside is not None and k == rounds_first:
            a, b, beside = lax.optimization_barrier((a, b, beside))
        blocks[-k] = a
        if k < n - n // 2:
            blocks[k] = b
    return blocks if beside is None else (blocks, beside)


def turned_dot(left, right):
    return lax.dot_general(left, right, (((1,), (1,)), ((), ())), preferred_element_type=F32)


def inverse_rms(wide):
    return lax.rsqrt(jnp.mean(wide * wide, axis=-1, keepdims=True) + EPSILON)


def vision_kernel(core_ref, patches_ref, column_ref, row_ref, gain_ref, weight_ref, out_ref):
    wide = patches_ref[...].astype(F32)
    normed = (wide * inverse_rms(wide) * gain_ref[...]).astype(BF16)
    query, keys, values = (
        turned_dot(normed, weight_ref[k]).astype(BF16) for k in range(3)
    )
    same = column_ref[...] == row_ref[...]
    for head in range(2):
        part = slice(head * HEAD_VIT, (head + 1) * HEAD_VIT)
        scores = turned_dot(query[:, part], keys[:, part])
        scores = jnp.where(same, scores * (1.0 / math.sqrt(HEAD_VIT)), -1e30)
        weights = jnp.exp(scores - jnp.max(scores, axis=-1, keepdims=True))
        probs = (weights / jnp.sum(weights, axis=-1, keepdims=True)).astype(BF16)
        context = lax.dot_general(
            values[:, part], probs, (((0,), (1,)), ((), ())), preferred_element_type=F32
        )
        place = pl.multiple_of(lax.rem(core_ref[0] + head, 2) * HEAD_VIT, 16)
        out_ref[pl.ds(place, HEAD_VIT), :] = context.astype(BF16)


def stack_kernel(*refs):
    for k, ref in enumerate(refs[:-1]):
        refs[-1][k] = ref[...]


def merge_kernel(n, *refs):
    contexts, mine = refs[:n], refs[n : 2 * n]
    other_ref, patches_ref, gain_ref, merger_hbm, slot_ref, audio_ref, out_ref = refs[2 * n : 2 * n + 7]
    context, weight, normed, merger, sem = refs[2 * n + 7 :]
    fetch = pltpu.make_async_copy(merger_hbm, merger, sem)
    fetch.start()
    for k in range(n):
        context[pl.ds(k * 2 * HEAD_VIT, 2 * HEAD_VIT), :] = contexts[k][...]
        weight[pl.ds(k * 2 * HEAD_VIT, HEAD_VIT), :] = mine[k][...]
        weight[pl.ds((2 * k + 1) * HEAD_VIT, HEAD_VIT), :] = other_ref[k]
    rows, d_vit = patches_ref.shape
    turned = context[...].T

    lanes = 128
    squares = jnp.zeros((rows, 1), F32)
    for j in range(d_vit // 256):
        columns = pl.ds(j * 256, 256)
        attended = jnp.dot(turned, weight[:, columns], preferred_element_type=F32)
        wide = (patches_ref[:, columns].astype(F32) + attended).astype(BF16).astype(F32)
        squares += jnp.sum(wide * wide, axis=-1, keepdims=True)
        normed[2 * j] = wide[:, :lanes]
        normed[2 * j + 1] = wide[:, lanes:]
    scale = lax.rsqrt(squares / d_vit + EPSILON)
    for j in range(d_vit // lanes):
        normed[j] = normed[j] * scale * gain_ref[:, pl.ds(j * lanes, lanes)]

    fetch.wait()
    video = jnp.zeros((rows // 4, merger.shape[0]), F32)
    for j in range(4):
        part = [normed[k, pl.ds(j, rows // 4, stride=4), :] for k in range(d_vit // lanes)]
        part = jnp.concatenate(part, axis=1).astype(BF16)
        video += turned_dot(part, merger[:, pl.ds(j * d_vit, d_vit)])
    video = video.astype(BF16)
    index = lax.broadcasted_iota(jnp.int32, (slot_ref.shape[0], rows // 4), 1)
    select = (slot_ref[...] == index).astype(F32).astype(BF16)
    placed = jnp.dot(select, video, preferred_element_type=F32)
    out_ref[...] = (placed + audio_ref[...].astype(F32)).astype(BF16)


def pick_kernel(target_ref, incoming_ref, out_ref):
    rows = lax.broadcasted_iota(jnp.int32, (out_ref.shape[0], incoming_ref.shape[0]), 0)
    pick = (rows == target_ref[...]).astype(F32).astype(BF16)
    out_ref[...] = jnp.dot(pick, incoming_ref[...], preferred_element_type=F32).astype(BF16)


def ffn_kernel(n, shifts, units, place_ref, *refs):
    blocks, gain_ref, whole_hbm, out_ref, own_ref = refs[:n], refs[n], refs[n + 1], refs[n + 2], refs[n + 3]
    whole, normed, both, hidden, sems = refs[n + 4 :]
    features, width = whole.shape
    tile = 256
    low = 2 * units // tile * tile
    tiles = low // tile

    def part(j):
        columns = pl.ds(pl.multiple_of(j * tile, tile), tile)
        return pltpu.make_async_copy(whole_hbm.at[:, columns], whole.at[:, columns], sems.at[j])

    rest = pltpu.make_async_copy(
        whole_hbm.at[:, pl.ds(low, width - low)], whole.at[:, pl.ds(low, width - low)], sems.at[tiles]
    )

    @pl.loop(0, tiles)
    def _(j):
        part(j).start()

    rest.start()

    rows, chunk = blocks[0].shape
    squares = jnp.zeros((rows, 1), F32)
    for block in blocks:
        wide = block[...].astype(F32)
        squares += jnp.sum(wide * wide, axis=-1, keepdims=True)
    scale = lax.rsqrt(squares / features + EPSILON)
    own = own_ref.shape[1]
    first = pl.multiple_of(place_ref[0] * own, own)
    for shift, block in zip(shifts, blocks):
        at = lax.rem(place_ref[0] + shift + n, n)
        gain = gain_ref[at]
        normed[at] = (block[...].astype(F32) * scale * gain).astype(BF16)
        own_ref[at] = block[pl.ds(first, own), :]

    def product(columns):
        total = jnp.dot(normed[0], whole[pl.ds(0, chunk), columns], preferred_element_type=F32)
        for k in range(1, n):
            total += jnp.dot(normed[k], whole[pl.ds(k * chunk, chunk), columns], preferred_element_type=F32)
        both[:, columns] = total

    @pl.loop(0, tiles)
    def _(j):
        part(j).wait()
        product(pl.ds(pl.multiple_of(j * tile, tile), tile))

    rest.wait()
    lead = 2 * units - low
    tail = (lead + 127) // 128 * 128
    product(pl.ds(low, tail))

    step = 64

    @pl.loop(0, rows // step)
    def _(j):
        here = pl.ds(pl.multiple_of(j * step, step), step)
        gate = both[here, pl.ds(0, units)]
        upward = both[here, pl.ds(units, units)]
        value = gate * (1.0 / (1.0 + jnp.exp(-gate))) * upward
        hidden[here, pl.ds(0, lead)] = jnp.zeros((step, lead), BF16)
        hidden[here, pl.ds(lead, units)] = value.astype(BF16)

    @pl.loop(0, features // tile)
    def _(j):
        here = pl.ds(pl.multiple_of(j * tile, tile), tile)
        out_ref[:, here] = turned_dot(hidden[...], whole[here, pl.ds(low, width - low)]).astype(BF16)


def call(kernel, out_shape, specs, flops, scratch=(), mib=48):
    def run(*args):
        moved = sum(a.size * a.dtype.itemsize for a in args)
        return pl.pallas_call(
            kernel,
            out_shape=out_shape,
            in_specs=specs,
            out_specs=jax.tree.map(lambda _: pl.BlockSpec(memory_space=VMEM), out_shape),
            scratch_shapes=scratch,
            compiler_params=pltpu.CompilerParams(vmem_limit_bytes=mib << 20),
            cost_estimate=pl.CostEstimate(flops=flops, bytes_accessed=moved, transcendentals=0),
        )(*args)

    return run


def body(
    patches,
    window_ids,
    vit_gain,
    qkv_weight,
    out_weight,
    merge_gain,
    merger_weight,
    audio,
    span_lengths,
    span_time,
    llm_gain,
    gate_weight,
    up_weight,
    down_weight,
):
    patch_count, d_vit = patches.shape
    n = lax.axis_size("tensor")
    owner_count = lax.axis_size("dp")
    owner = lax.axis_index("dp")
    plane = lax.axis_index("tensor")
    core = lax.rem(owner, 2)
    units = gate_weight.shape[1]
    vmem = pl.BlockSpec(memory_space=VMEM)
    smem = pl.BlockSpec(memory_space=SMEM)
    hbm = pl.BlockSpec(memory_space=pl.ANY)

    windows = window_ids[0]
    context = call(
        vision_kernel,
        jax.ShapeDtypeStruct((2 * HEAD_VIT, patch_count), BF16),
        [smem] + [vmem] * 5,
        2 * patch_count * (3 * d_vit * 160 + 4 * patch_count * HEAD_VIT),
    )(
        core.reshape(1),
        patches,
        windows[:, None],
        windows[None, :],
        vit_gain[None, :],
        jnp.swapaxes(qkv_weight, 1, 2),
    )

    own_head = lax.dynamic_slice_in_dim(out_weight, core * HEAD_VIT, HEAD_VIT, 0)
    heads, context = ring_blocks(own_head, "tensor", context)
    order = sorted(heads)
    mine = [heads[k] for k in order]
    swap = [(i, i ^ 1) for i in range(owner_count)]
    laid = call(stack_kernel, jax.ShapeDtypeStruct((n, *own_head.shape), BF16), [vmem] * n, 0)(*mine)
    other = lax.ppermute(laid, "dp", swap)

    stacked = jnp.concatenate([gate_weight, up_weight, down_weight.T], axis=1)
    whole = lax.all_gather(stacked, "dp", axis=0, tiled=True)

    context, laid = lax.optimization_barrier((context, laid))
    got = ring_blocks(context, "tensor")

    video_rows = patch_count // 4
    seq_count = video_rows + audio.shape[0]
    capacity = 2 * seq_count // owner_count
    sent_lengths = span_lengths[owner]
    starts = jnp.cumsum(sent_lengths) - sent_lengths
    slot_index = jnp.arange(capacity, dtype=jnp.int32)
    row_of_slot = jnp.where(
        slot_index[None, :] < sent_lengths[:, None], starts[:, None] + slot_index[None, :], -1
    ).reshape(-1)
    row = jnp.arange(seq_count, dtype=jnp.int32)
    select = (row_of_slot[:, None] == row[None, video_rows:]).astype(BF16)
    from_audio = jnp.dot(select, audio, preferred_element_type=F32).astype(BF16)
    slots = owner_count * capacity
    width = audio.shape[1]
    outgoing = call(
        functools.partial(merge_kernel, n),
        jax.ShapeDtypeStruct((slots, width), BF16),
        [vmem] * (2 * n + 3) + [hbm, vmem, vmem],
        2 * patch_count * d_vit * (d_vit + width),
        scratch=[
            pltpu.VMEM((d_vit, patch_count), BF16),
            pltpu.VMEM((d_vit, d_vit), BF16),
            pltpu.VMEM((d_vit // 128, patch_count, 128), F32),
            pltpu.VMEM(merger_weight.shape[::-1], BF16),
            pltpu.SemaphoreType.DMA,
        ],
    )(
        *[got[k] for k in order],
        *mine,
        other,
        patches,
        merge_gain[None, :],
        merger_weight.T,
        row_of_slot[:, None],
        from_audio,
    )
    incoming = lax.all_to_all(
        outgoing.reshape(owner_count, capacity, width), "dp", split_axis=0, concat_axis=0, tiled=True
    ).reshape(slots, width)
    taken_lengths = span_lengths[:, owner]
    arrival = span_time[owner]
    earlier = arrival[:, None] < arrival[None, :]
    offsets = jnp.sum(jnp.where(earlier, taken_lengths[:, None], 0), axis=0)
    target = jnp.where(
        slot_index[None, :] < taken_lengths[:, None], offsets[:, None] + slot_index[None, :], -1
    ).reshape(1, -1)
    sequence = call(
        pick_kernel,
        jax.ShapeDtypeStruct((seq_count, width), BF16),
        [vmem] * 2,
        2 * slots * seq_count * width,
    )(target, incoming)

    got = ring_blocks(sequence, "tensor")
    features = n * width
    low = 2 * units // 256 * 256
    tail = (2 * units - low + 127) // 128 * 128
    own_count = seq_count // n
    terms, own_rows = call(
        functools.partial(ffn_kernel, n, tuple(order), units),
        (
            jax.ShapeDtypeStruct((seq_count, features), BF16),
            jax.ShapeDtypeStruct((n, own_count, width), BF16),
        ),
        [smem] + [vmem] * (n + 1) + [hbm],
        6 * seq_count * features * units,
        scratch=[
            pltpu.VMEM((features, 3 * units), BF16),
            pltpu.VMEM((n, seq_count, width), BF16),
            pltpu.VMEM((seq_count, low + tail), F32),
            pltpu.VMEM((seq_count, 3 * units - low), BF16),
            pltpu.SemaphoreType.DMA((low // 256 + 1,)),
        ],
        mib=60,
    )(
        plane.reshape(1),
        *[got[k] for k in order],
        llm_gain.reshape(n, 1, width),
        whole,
    )
    summed = lax.psum_scatter(terms, "tensor", scatter_dimension=0, tiled=True).astype(F32)
    own_rows = jnp.moveaxis(own_rows, 0, 1).reshape(own_count, features)
    return (own_rows.astype(F32) + summed).astype(BF16)


def solution(mesh):
    return jax.shard_map(
        body,
        mesh=mesh,
        in_specs=(
            P("dp", None),
            P("dp", None),
            P(),
            P(None, None, "tensor"),
            P("tensor", None),
            P(),
            P(None, "tensor"),
            P("dp", "tensor"),
            P(),
            P(),
            P(),
            P("dp", "tensor"),
            P("dp", "tensor"),
            P("tensor", "dp"),
        ),
        out_specs=P(("dp", "tensor"), None),
        check_vma=False,
    )
```

```python
import functools
import math

import jax
import jax.numpy as jnp
from jax import lax
from jax.experimental import pallas as pl
from jax.experimental.pallas import tpu as pltpu
from jax.sharding import PartitionSpec as P

HEAD_VIT = 80
EPSILON = 1e-06
VMEM = pltpu.MemorySpace.VMEM
SMEM = pltpu.MemorySpace.SMEM
BF16 = jnp.bfloat16
F32 = jnp.float32


def shifted(axis, step):
    n = lax.axis_size(axis)
    return [(i, (i + step) % n) for i in range(n)]


def ring_blocks(x, axis):
    n = lax.axis_size(axis)
    blocks = {0: x}
    a = b = x
    for k in range(1, n // 2 + 1):
        a = lax.ppermute(a, axis, shifted(axis, 1))
        blocks[-k] = a
        if k < n - n // 2:
            b = lax.ppermute(b, axis, shifted(axis, -1))
            blocks[k] = b
    return blocks


def turned_dot(left, right):
    return lax.dot_general(left, right, (((1,), (1,)), ((), ())), preferred_element_type=F32)


def inverse_rms(wide):
    return lax.rsqrt(jnp.mean(wide * wide, axis=-1, keepdims=True) + EPSILON)


def vision_kernel(core_ref, patches_ref, column_ref, row_ref, gain_ref, weight_ref, out_ref):
    wide = patches_ref[...].astype(F32)
    normed = (wide * inverse_rms(wide) * gain_ref[...]).astype(BF16)
    query, keys, values = (
        turned_dot(normed, weight_ref[k]).astype(BF16) for k in range(3)
    )
    same = column_ref[...] == row_ref[...]
    for head in range(2):
        part = slice(head * HEAD_VIT, (head + 1) * HEAD_VIT)
        scores = turned_dot(query[:, part], keys[:, part])
        scores = jnp.where(same, scores * (1.0 / math.sqrt(HEAD_VIT)), -1e30)
        weights = jnp.exp(scores - jnp.max(scores, axis=-1, keepdims=True))
        probs = (weights / jnp.sum(weights, axis=-1, keepdims=True)).astype(BF16)
        context = lax.dot_general(
            values[:, part], probs, (((0,), (1,)), ((), ())), preferred_element_type=F32
        )
        place = pl.multiple_of(lax.rem(core_ref[0] + head, 2) * HEAD_VIT, 16)
        out_ref[pl.ds(place, HEAD_VIT), :] = context.astype(BF16)


def lay(into, at, wide):
    rows, columns = wide.shape
    for j in range(columns // 128):
        into[pl.ds(at + j * rows, rows), :] = wide[:, pl.ds(j * 128, 128)]


def spread(into, at, tall, start, rows):
    for j in range(into.shape[1] // 128):
        into[pl.ds(at, rows), pl.ds(j * 128, 128)] = tall[pl.ds(start + j * rows, rows), :]


def pack_kernel(context_ref, above_ref, below_ref, up_ref, down_ref):
    split = context_ref.size // 128
    for out_ref, block_ref in ((up_ref, above_ref), (down_ref, below_ref)):
        lay(out_ref, 0, context_ref)
        lay(out_ref, split, block_ref)


def stack_kernel(wide_count, *refs):
    blocks, out_ref = refs[:-1], refs[-1]
    rows = out_ref.shape[1]
    for k, ref in enumerate(blocks):
        if k < wide_count:
            lay(out_ref.at[k], 0, ref)
        else:
            out_ref[k] = ref[pl.ds(ref.shape[0] - rows, rows), :]


def merge_kernel(n, *refs):
    contexts, wide, tall = refs[:n], refs[n : n + 3], refs[n + 3 : 2 * n]
    other_ref, last_ref = refs[2 * n : 2 * n + 2]
    patches_ref, gain_ref, merger_hbm, slot_ref, audio_ref, out_ref = refs[2 * n + 2 : 2 * n + 8]
    context, weight, normed, merger, sem = refs[2 * n + 8 :]
    fetch = pltpu.make_async_copy(merger_hbm, merger, sem)
    fetch.start()
    group = 2 * HEAD_VIT
    split = group * context.shape[1] // 128
    for k in range(n):
        spread(context, k * group, contexts[k], 0, group)
        if k < 3:
            weight[pl.ds(k * group, HEAD_VIT), :] = wide[k][...]
        else:
            spread(weight, k * group, tall[k - 3], split, HEAD_VIT)
        if k < n - 1:
            spread(weight, k * group + HEAD_VIT, other_ref.at[k], 0, HEAD_VIT)
        else:
            spread(weight, k * group + HEAD_VIT, last_ref, split, HEAD_VIT)
    rows, d_vit = patches_ref.shape
    turned = context[...].T

    lanes = 128
    squares = jnp.zeros((rows, 1), F32)
    for j in range(d_vit // 256):
        columns = pl.ds(j * 256, 256)
        attended = jnp.dot(turned, weight[:, columns], preferred_element_type=F32)
        wide = (patches_ref[:, columns].astype(F32) + attended).astype(BF16).astype(F32)
        squares += jnp.sum(wide * wide, axis=-1, keepdims=True)
        normed[2 * j] = wide[:, :lanes]
        normed[2 * j + 1] = wide[:, lanes:]
    scale = lax.rsqrt(squares / d_vit + EPSILON)
    for j in range(d_vit // lanes):
        normed[j] = normed[j] * scale * gain_ref[:, pl.ds(j * lanes, lanes)]

    fetch.wait()
    video = jnp.zeros((rows // 4, merger.shape[0]), F32)
    for j in range(4):
        part = [normed[k, pl.ds(j, rows // 4, stride=4), :] for k in range(d_vit // lanes)]
        part = jnp.concatenate(part, axis=1).astype(BF16)
        video += turned_dot(part, merger[:, pl.ds(j * d_vit, d_vit)])
    video = video.astype(BF16)
    index = lax.broadcasted_iota(jnp.int32, (slot_ref.shape[0], rows // 4), 1)
    select = (slot_ref[...] == index).astype(F32).astype(BF16)
    placed = jnp.dot(select, video, preferred_element_type=F32)
    out_ref[...] = (placed + audio_ref[...].astype(F32)).astype(BF16)


def pick_kernel(n, target_ref, incoming_ref, *outs):
    count = len(outs)
    for k, out_ref in enumerate(outs):
        run = out_ref.shape[0] // n
        row = lax.broadcasted_iota(jnp.int32, (out_ref.shape[0], incoming_ref.shape[0]), 0)
        position = row // run * (run * count) + k * run + row % run
        pick = (position == target_ref[...]).astype(F32).astype(BF16)
        out_ref[...] = jnp.dot(pick, incoming_ref[...], preferred_element_type=F32).astype(BF16)


def ffn_kernel(n, shifts, units, place_ref, *refs):
    blocks, gain_ref, whole_hbm, out_ref, own_ref = refs[:n], refs[n], refs[n + 1], refs[n + 2], refs[n + 3]
    whole, normed, both, hidden, sems = refs[n + 4 :]
    features, width = whole.shape
    tile = 256
    low = 2 * units // tile * tile
    tiles = low // tile

    def part(j):
        columns = pl.ds(pl.multiple_of(j * tile, tile), tile)
        return pltpu.make_async_copy(whole_hbm.at[:, columns], whole.at[:, columns], sems.at[j])

    rest = pltpu.make_async_copy(
        whole_hbm.at[:, pl.ds(low, width - low)], whole.at[:, pl.ds(low, width - low)], sems.at[tiles]
    )

    @pl.loop(0, tiles)
    def _(j):
        part(j).start()

    rest.start()

    rows, chunk = blocks[0].shape
    squares = jnp.zeros((rows, 1), F32)
    for block in blocks:
        wide = block[...].astype(F32)
        squares += jnp.sum(wide * wide, axis=-1, keepdims=True)
    scale = lax.rsqrt(squares / features + EPSILON)
    own = own_ref.shape[1]
    first = pl.multiple_of(place_ref[0] * own, own)
    for shift, block in zip(shifts, blocks):
        at = lax.rem(place_ref[0] + shift + n, n)
        gain = gain_ref[at]
        normed[at] = (block[...].astype(F32) * scale * gain).astype(BF16)
        own_ref[at] = block[pl.ds(first, own), :]

    def product(columns):
        total = jnp.dot(normed[0], whole[pl.ds(0, chunk), columns], preferred_element_type=F32)
        for k in range(1, n):
            total += jnp.dot(normed[k], whole[pl.ds(k * chunk, chunk), columns], preferred_element_type=F32)
        both[:, columns] = total

    @pl.loop(0, tiles)
    def _(j):
        part(j).wait()
        product(pl.ds(pl.multiple_of(j * tile, tile), tile))

    rest.wait()
    lead = 2 * units - low
    tail = (lead + 127) // 128 * 128
    product(pl.ds(low, tail))

    step = 64

    @pl.loop(0, rows // step)
    def _(j):
        here = pl.ds(pl.multiple_of(j * step, step), step)
        gate = both[here, pl.ds(0, units)]
        upward = both[here, pl.ds(units, units)]
        value = gate * (1.0 / (1.0 + jnp.exp(-gate))) * upward
        hidden[here, pl.ds(0, lead)] = jnp.zeros((step, lead), BF16)
        hidden[here, pl.ds(lead, units)] = value.astype(BF16)

    @pl.loop(0, features // tile)
    def _(j):
        here = pl.ds(pl.multiple_of(j * tile, tile), tile)
        out_ref[:, here] = turned_dot(hidden[...], whole[here, pl.ds(low, width - low)]).astype(BF16)


def call(kernel, out_shape, specs, flops, scratch=(), mib=48):
    def run(*args):
        moved = sum(a.size * a.dtype.itemsize for a in args)
        return pl.pallas_call(
            kernel,
            out_shape=out_shape,
            in_specs=specs,
            out_specs=jax.tree.map(lambda _: pl.BlockSpec(memory_space=VMEM), out_shape),
            scratch_shapes=scratch,
            compiler_params=pltpu.CompilerParams(vmem_limit_bytes=mib << 20),
            cost_estimate=pl.CostEstimate(flops=flops, bytes_accessed=moved, transcendentals=0),
        )(*args)

    return run


def body(
    patches,
    window_ids,
    vit_gain,
    qkv_weight,
    out_weight,
    merge_gain,
    merger_weight,
    audio,
    span_lengths,
    span_time,
    llm_gain,
    gate_weight,
    up_weight,
    down_weight,
):
    patch_count, d_vit = patches.shape
    n = lax.axis_size("tensor")
    owner_count = lax.axis_size("dp")
    owner = lax.axis_index("dp")
    plane = lax.axis_index("tensor")
    core = lax.rem(owner, 2)
    units = gate_weight.shape[1]
    vmem = pl.BlockSpec(memory_space=VMEM)
    smem = pl.BlockSpec(memory_space=SMEM)
    hbm = pl.BlockSpec(memory_space=pl.ANY)

    windows = window_ids[0]
    context = call(
        vision_kernel,
        jax.ShapeDtypeStruct((2 * HEAD_VIT, patch_count), BF16),
        [smem] + [vmem] * 5,
        2 * patch_count * (3 * d_vit * 160 + 4 * patch_count * HEAD_VIT),
    )(
        core.reshape(1),
        patches,
        windows[:, None],
        windows[None, :],
        vit_gain[None, :],
        jnp.swapaxes(qkv_weight, 1, 2),
    )

    group = 2 * HEAD_VIT
    own_head = lax.dynamic_slice_in_dim(out_weight, core * HEAD_VIT, HEAD_VIT, 0)
    above = lax.ppermute(own_head, "tensor", shifted("tensor", 1))
    below = lax.ppermute(own_head, "tensor", shifted("tensor", -1))
    split, block_rows = group * patch_count // 128, HEAD_VIT * d_vit // 128
    payload = jax.ShapeDtypeStruct((split + block_rows, 128), BF16)
    up, down = call(pack_kernel, (payload, payload), [vmem] * 3, 0)(context, above, below)
    ups, downs = [up], [down]
    for k in range(1, n // 2):
        ups.append(lax.ppermute(ups[-1], "tensor", shifted("tensor", 1)))
        away = downs[-1] if k < n // 2 - 1 else downs[-1][:split]
        downs.append(lax.ppermute(away, "tensor", shifted("tensor", -1)))
    ups.append(lax.ppermute(ups[-1][:split], "tensor", shifted("tensor", 1)))
    contexts = [up]
    tall = []
    for k in range(1, n // 2 + 1):
        contexts.append(ups[k])
        if k < n // 2:
            contexts.append(downs[k])
            tall.append(ups[k])
        if k < n // 2 - 1:
            tall.append(downs[k])
    swap = [(i, i ^ 1) for i in range(owner_count)]
    laid = call(
        functools.partial(stack_kernel, 3),
        jax.ShapeDtypeStruct((n - 1, block_rows, 128), BF16),
        [vmem] * (n - 1),
        0,
    )(own_head, above, below, *tall[:-1])
    other = lax.ppermute(laid, "dp", swap)
    last = lax.ppermute(tall[-1], "dp", swap)

    stacked = jnp.concatenate([gate_weight, up_weight, down_weight.T], axis=1)
    whole = lax.all_gather(stacked, "dp", axis=0, tiled=True)

    video_rows = patch_count // 4
    seq_count = video_rows + audio.shape[0]
    capacity = 2 * seq_count // owner_count
    sent_lengths = span_lengths[owner]
    starts = jnp.cumsum(sent_lengths) - sent_lengths
    slot_index = jnp.arange(capacity, dtype=jnp.int32)
    row_of_slot = jnp.where(
        slot_index[None, :] < sent_lengths[:, None], starts[:, None] + slot_index[None, :], -1
    ).reshape(-1)
    row = jnp.arange(seq_count, dtype=jnp.int32)
    select = (row_of_slot[:, None] == row[None, video_rows:]).astype(BF16)
    from_audio = jnp.dot(select, audio, preferred_element_type=F32).astype(BF16)
    slots = owner_count * capacity
    width = audio.shape[1]
    outgoing = call(
        functools.partial(merge_kernel, n),
        jax.ShapeDtypeStruct((slots, width), BF16),
        [vmem] * (2 * n + 4) + [hbm, vmem, vmem],
        2 * patch_count * d_vit * (d_vit + width),
        scratch=[
            pltpu.VMEM((d_vit, patch_count), BF16),
            pltpu.VMEM((d_vit, d_vit), BF16),
            pltpu.VMEM((d_vit // 128, patch_count, 128), F32),
            pltpu.VMEM(merger_weight.shape[::-1], BF16),
            pltpu.SemaphoreType.DMA,
        ],
    )(
        *contexts,
        own_head,
        above,
        below,
        *tall,
        other,
        last,
        patches,
        merge_gain[None, :],
        merger_weight.T,
        row_of_slot[:, None],
        from_audio,
    )
    incoming = lax.all_to_all(
        outgoing.reshape(owner_count, capacity, width), "dp", split_axis=0, concat_axis=0, tiled=True
    ).reshape(slots, width)
    taken_lengths = span_lengths[:, owner]
    arrival = span_time[owner]
    earlier = arrival[:, None] < arrival[None, :]
    offsets = jnp.sum(jnp.where(earlier, taken_lengths[:, None], 0), axis=0)
    target = jnp.where(
        slot_index[None, :] < taken_lengths[:, None], offsets[:, None] + slot_index[None, :], -1
    ).reshape(1, -1)
    parts = 2
    part_rows = seq_count // parts
    sequence = call(
        functools.partial(pick_kernel, n),
        (jax.ShapeDtypeStruct((part_rows, width), BF16),) * parts,
        [vmem] * 2,
        2 * slots * seq_count * width,
    )(target, incoming)

    features = n * width
    low = 2 * units // 256 * 256
    tail = (2 * units - low + 127) // 128 * 128
    own_count = part_rows // n
    results = []
    waiting = list(sequence)
    for k in range(parts):
        got = ring_blocks(waiting[k], "tensor")
        order = sorted(got)
        blocks = [got[j] for j in order]
        if k + 1 < parts:
            waiting[k + 1], blocks = lax.optimization_barrier((waiting[k + 1], blocks))
        terms, own_rows = call(
            functools.partial(ffn_kernel, n, tuple(order), units),
            (
                jax.ShapeDtypeStruct((part_rows, features), BF16),
                jax.ShapeDtypeStruct((n, own_count, width), BF16),
            ),
            [smem] + [vmem] * (n + 1) + [hbm],
            6 * part_rows * features * units,
            scratch=[
                pltpu.VMEM((features, 3 * units), BF16),
                pltpu.VMEM((n, part_rows, width), BF16),
                pltpu.VMEM((part_rows, low + tail), F32),
                pltpu.VMEM((part_rows, 3 * units - low), BF16),
                pltpu.SemaphoreType.DMA((low // 256 + 1,)),
            ],
            mib=60,
        )(plane.reshape(1), *blocks, llm_gain.reshape(n, 1, width), whole)
        summed = lax.psum_scatter(terms, "tensor", scatter_dimension=0, tiled=True).astype(F32)
        own_rows = jnp.moveaxis(own_rows, 0, 1).reshape(own_count, features)
        results.append((own_rows.astype(F32) + summed).astype(BF16))
    return jnp.concatenate(results, axis=0)


def solution(mesh):
    return jax.shard_map(
        body,
        mesh=mesh,
        in_specs=(
            P("dp", None),
            P("dp", None),
            P(),
            P(None, None, "tensor"),
            P("tensor", None),
            P(),
            P(None, "tensor"),
            P("dp", "tensor"),
            P(),
            P(),
            P(),
            P("dp", "tensor"),
            P("dp", "tensor"),
            P("tensor", "dp"),
        ),
        out_specs=P(("dp", "tensor"), None),
        check_vma=False,
    )
```

```python
import functools
import math

import jax
import jax.numpy as jnp
from jax import lax
from jax.experimental import pallas as pl
from jax.experimental.pallas import tpu as pltpu
from jax.sharding import PartitionSpec as P

HEAD_VIT = 80
EPSILON = 1e-06
VMEM = pltpu.MemorySpace.VMEM
SMEM = pltpu.MemorySpace.SMEM
HBM = pltpu.MemorySpace.HBM
BF16 = jnp.bfloat16
F32 = jnp.float32


def shifted(axis, step):
    n = lax.axis_size(axis)
    return [(i, (i + step) % n) for i in range(n)]


def ring_blocks(x, axis):
    n = lax.axis_size(axis)
    blocks = {0: x}
    a = b = x
    for k in range(1, n // 2 + 1):
        a = lax.ppermute(a, axis, shifted(axis, 1))
        blocks[-k] = a
        if k < n - n // 2:
            b = lax.ppermute(b, axis, shifted(axis, -1))
            blocks[k] = b
    return blocks


def turned_dot(left, right):
    return lax.dot_general(left, right, (((1,), (1,)), ((), ())), preferred_element_type=F32)


def inverse_rms(wide):
    return lax.rsqrt(jnp.mean(wide * wide, axis=-1, keepdims=True) + EPSILON)


def vision_kernel(core_ref, patches_ref, column_ref, row_ref, gain_ref, weight_ref, out_ref):
    wide = patches_ref[...].astype(F32)
    normed = (wide * inverse_rms(wide) * gain_ref[...]).astype(BF16)
    query, keys, values = (
        turned_dot(normed, weight_ref[k]).astype(BF16) for k in range(3)
    )
    same = column_ref[...] == row_ref[...]
    for head in range(2):
        part = slice(head * HEAD_VIT, (head + 1) * HEAD_VIT)
        scores = turned_dot(query[:, part], keys[:, part])
        scores = jnp.where(same, scores * (1.0 / math.sqrt(HEAD_VIT)), -1e30)
        weights = jnp.exp(scores - jnp.max(scores, axis=-1, keepdims=True))
        probs = (weights / jnp.sum(weights, axis=-1, keepdims=True)).astype(BF16)
        context = lax.dot_general(
            values[:, part], probs, (((0,), (1,)), ((), ())), preferred_element_type=F32
        )
        place = pl.multiple_of(lax.rem(core_ref[0] + head, 2) * HEAD_VIT, 16)
        out_ref[pl.ds(place, HEAD_VIT), :] = context.astype(BF16)


def lay(into, at, wide):
    rows, columns = wide.shape
    for j in range(columns // 128):
        into[pl.ds(at + j * rows, rows), :] = wide[:, pl.ds(j * 128, 128)]


def spread(into, at, tall, start, rows):
    for j in range(into.shape[1] // 128):
        into[pl.ds(at, rows), pl.ds(j * 128, 128)] = tall[pl.ds(start + j * rows, rows), :]


def pack_kernel(context_ref, above_ref, below_ref, up_ref, down_ref):
    split = context_ref.size // 128
    for out_ref, block_ref in ((up_ref, above_ref), (down_ref, below_ref)):
        lay(out_ref, 0, context_ref)
        lay(out_ref, split, block_ref)


def stack_kernel(wide_count, *refs):
    blocks, out_ref = refs[:-1], refs[-1]
    rows = out_ref.shape[1]
    for k, ref in enumerate(blocks):
        if k < wide_count:
            lay(out_ref.at[k], 0, ref)
        else:
            out_ref[k] = ref[pl.ds(ref.shape[0] - rows, rows), :]


def project_kernel(n, *refs):
    count = n + 4
    sources, out_ref, sems = refs[:count], refs[count], refs[-1]
    places, (context, weight) = refs[count + 1 : 2 * count + 1], refs[2 * count + 1 : 2 * count + 3]
    fetch = [
        pltpu.make_async_copy(source, place, sems.at[k])
        for k, (source, place) in enumerate(zip(sources, places))
    ]
    for copy in fetch:
        copy.start()
    payloads, wide, (other, patches) = places[: n - 1], places[n - 1 : n + 2], places[n + 2 :]
    group = 2 * HEAD_VIT
    split = group * context.shape[1] // 128
    for k in range(n - 1):
        fetch[k].wait()
        spread(context, k * group, payloads[k], 0, group)
    for k in range(3):
        fetch[n - 1 + k].wait()
        weight[pl.ds(k * group, HEAD_VIT), :] = wide[k][...]
    for k in range(3, n - 1):
        spread(weight, k * group, payloads[k - 2], split, HEAD_VIT)
    turned = context[...].T
    fetch[n + 2].wait()
    for k in range(n - 1):
        spread(weight, k * group + HEAD_VIT, other.at[k], 0, HEAD_VIT)
    fetch[n + 3].wait()

    @pl.loop(0, out_ref.shape[1] // 256)
    def _(j):
        columns = pl.ds(pl.multiple_of(j * 256, 256), 256)
        attended = jnp.dot(turned, weight[:, columns], preferred_element_type=F32)
        out_ref[:, columns] = patches[:, columns].astype(F32) + attended


def merge_kernel(*refs):
    context_ref, mine_ref, last_ref, sofar_ref, gain_ref, merger_hbm, slot_ref, audio_hbm, out_ref = refs[:9]
    context, weight, normed, merger, audio, sems = refs[9:]
    fetch = [
        pltpu.make_async_copy(merger_hbm, merger, sems.at[0]),
        pltpu.make_async_copy(audio_hbm, audio, sems.at[1]),
    ]
    for copy in fetch:
        copy.start()
    rows, d_vit = sofar_ref.shape
    group = 2 * HEAD_VIT
    split = group * rows // 128
    spread(context, 0, context_ref, 0, group)
    spread(weight, 0, mine_ref, split, HEAD_VIT)
    spread(weight, HEAD_VIT, last_ref, split, HEAD_VIT)
    turned = context[...].T
    lanes = 128
    squares = jnp.zeros((rows, 1), F32)
    for j in range(d_vit // 256):
        columns = pl.ds(j * 256, 256)
        attended = jnp.dot(turned, weight[:, columns], preferred_element_type=F32)
        wide = (sofar_ref[:, columns] + attended).astype(BF16).astype(F32)
        squares += jnp.sum(wide * wide, axis=-1, keepdims=True)
        normed[2 * j] = wide[:, :lanes]
        normed[2 * j + 1] = wide[:, lanes:]
    scale = lax.rsqrt(squares / d_vit + EPSILON)
    for j in range(d_vit // lanes):
        normed[j] = normed[j] * scale * gain_ref[:, pl.ds(j * lanes, lanes)]

    fetch[0].wait()
    video = jnp.zeros((rows // 4, merger.shape[0]), F32)
    for j in range(4):
        part = [normed[k, pl.ds(j, rows // 4, stride=4), :] for k in range(d_vit // lanes)]
        part = jnp.concatenate(part, axis=1).astype(BF16)
        video += turned_dot(part, merger[:, pl.ds(j * d_vit, d_vit)])
    video = video.astype(BF16)
    index = lax.broadcasted_iota(jnp.int32, (slot_ref.shape[0], rows // 4), 1)
    select = (slot_ref[...] == index).astype(F32).astype(BF16)
    placed = jnp.dot(select, video, preferred_element_type=F32)
    fetch[1].wait()
    out_ref[...] = (placed + audio[...].astype(F32)).astype(BF16)


def pick_kernel(target_ref, incoming_ref, out_ref):
    row = lax.broadcasted_iota(jnp.int32, (out_ref.shape[0], incoming_ref.shape[0]), 0)
    pick = (row == target_ref[...]).astype(F32).astype(BF16)
    out_ref[...] = jnp.dot(pick, incoming_ref[...], preferred_element_type=F32).astype(BF16)


def gate_kernel(n, shifts, units, place_ref, *refs):
    sources, gain_ref, whole_hbm, hidden_ref, own_ref = refs[:n], refs[n], refs[n + 1], refs[n + 2], refs[n + 3]
    blocks, whole, normed, sems = refs[n + 4 :]
    features = whole.shape[0]
    rows, chunk = blocks.shape[1:]
    apart = whole.shape[1] - units
    bring, fetch, places = [], [], []
    for j, shift in enumerate(shifts):
        at = lax.rem(place_ref[0] + shift + n, n)
        places.append(at)
        bring.append(pltpu.make_async_copy(sources[j], blocks.at[j], sems.at[n + j]))
        source = whole_hbm.at[pl.ds(pl.multiple_of(at * chunk, 16), chunk), :]
        fetch.append(pltpu.make_async_copy(source, whole.at[pl.ds(j * chunk, chunk), :], sems.at[j]))
    for copy in bring + fetch:
        copy.start()
    squares = jnp.zeros((rows, 1), F32)
    for j in range(n):
        bring[j].wait()
        wide = blocks[j].astype(F32)
        squares += jnp.sum(wide * wide, axis=-1, keepdims=True)
    scale = lax.rsqrt(squares / features + EPSILON)
    own = own_ref.shape[1]
    first = pl.multiple_of(place_ref[0] * own, own)
    for j in range(n):
        gain = gain_ref[places[j]]
        normed[:, pl.ds(j * chunk, chunk)] = (blocks[j].astype(F32) * scale * gain).astype(BF16)
        own_ref[places[j]] = blocks[j, pl.ds(first, own), :]
    for copy in fetch:
        copy.wait()

    def step(start, width):
        gate = jnp.dot(normed[...], whole[:, pl.ds(start, width)], preferred_element_type=F32)
        upward = jnp.dot(normed[...], whole[:, pl.ds(apart + start, width)], preferred_element_type=F32)
        value = gate * (1.0 / (1.0 + jnp.exp(-gate))) * upward
        hidden_ref[:, pl.ds(start, width)] = value.astype(BF16)

    tile = 256

    @pl.loop(0, units // tile)
    def _(j):
        step(pl.multiple_of(j * tile, tile), tile)

    step(units // tile * tile, units % tile)


def down_kernel(hidden_ref, weight_hbm, out_hbm, weight, out, sems):
    tile = 256
    tiles = weight.shape[0] // tile

    def here(j):
        return pl.ds(pl.multiple_of(j * tile, tile), tile)

    def part(j):
        return pltpu.make_async_copy(weight_hbm.at[here(j), :], weight.at[here(j), :], sems.at[j])

    def result(j):
        return pltpu.make_async_copy(out.at[:, here(j)], out_hbm.at[:, here(j)], sems.at[tiles + j])

    @pl.loop(0, tiles)
    def _(j):
        part(j).start()

    @pl.loop(0, tiles)
    def _(j):
        part(j).wait()
        out[:, here(j)] = turned_dot(hidden_ref[...], weight[here(j), :]).astype(BF16)
        result(j).start()

    @pl.loop(0, tiles)
    def _(j):
        result(j).wait()


def call(kernel, out_shape, specs, flops, scratch=(), mib=16, out_space=VMEM):
    def run(*args):
        moved = sum(a.size * a.dtype.itemsize for a in args)
        return pl.pallas_call(
            kernel,
            out_shape=out_shape,
            in_specs=specs,
            out_specs=jax.tree.map(lambda _: pl.BlockSpec(memory_space=out_space), out_shape),
            scratch_shapes=scratch,
            compiler_params=pltpu.CompilerParams(vmem_limit_bytes=mib << 20),
            cost_estimate=pl.CostEstimate(flops=flops, bytes_accessed=moved, transcendentals=0),
        )(*args)

    return run


def body(
    patches,
    window_ids,
    vit_gain,
    qkv_weight,
    out_weight,
    merge_gain,
    merger_weight,
    audio,
    span_lengths,
    span_time,
    llm_gain,
    gate_weight,
    up_weight,
    down_weight,
):
    patch_count, d_vit = patches.shape
    n = lax.axis_size("tensor")
    owner_count = lax.axis_size("dp")
    owner = lax.axis_index("dp")
    plane = lax.axis_index("tensor")
    core = lax.rem(owner, 2)
    units = gate_weight.shape[1]
    vmem = pl.BlockSpec(memory_space=VMEM)
    smem = pl.BlockSpec(memory_space=SMEM)
    hbm = pl.BlockSpec(memory_space=HBM)

    windows = window_ids[0]
    context = call(
        vision_kernel,
        jax.ShapeDtypeStruct((2 * HEAD_VIT, patch_count), BF16),
        [smem] + [vmem] * 5,
        2 * patch_count * (3 * d_vit * 160 + 4 * patch_count * HEAD_VIT),
    )(
        core.reshape(1),
        patches,
        windows[:, None],
        windows[None, :],
        vit_gain[None, :],
        jnp.swapaxes(qkv_weight, 1, 2),
    )

    group = 2 * HEAD_VIT
    own_head = lax.dynamic_slice_in_dim(out_weight, core * HEAD_VIT, HEAD_VIT, 0)
    above = lax.ppermute(own_head, "tensor", shifted("tensor", 1))
    below = lax.ppermute(own_head, "tensor", shifted("tensor", -1))
    split, block_rows = group * patch_count // 128, HEAD_VIT * d_vit // 128
    payload = jax.ShapeDtypeStruct((split + block_rows, 128), BF16)
    up, down = call(pack_kernel, (payload, payload), [vmem] * 3, 0)(context, above, below)
    ups, downs = [up], [down]
    for k in range(1, n // 2):
        ups.append(lax.ppermute(ups[-1], "tensor", shifted("tensor", 1)))
        away = downs[-1] if k < n // 2 - 1 else downs[-1][:split]
        downs.append(lax.ppermute(away, "tensor", shifted("tensor", -1)))
    ups.append(lax.ppermute(ups[-1][:split], "tensor", shifted("tensor", 1)))
    contexts = [up]
    tall = []
    for k in range(1, n // 2 + 1):
        contexts.append(ups[k])
        if k < n // 2:
            contexts.append(downs[k])
            tall.append(ups[k])
        if k < n // 2 - 1:
            tall.append(downs[k])
    swap = [(i, i ^ 1) for i in range(owner_count)]
    laid = call(
        functools.partial(stack_kernel, 3),
        jax.ShapeDtypeStruct((n - 1, block_rows, 128), BF16),
        [vmem] * (n - 1),
        0,
    )(own_head, above, below, *tall[:-1])
    other = lax.ppermute(laid, "dp", swap)
    last = lax.ppermute(tall[-1], "dp", swap)

    gap = -units % 128
    stacked = jnp.concatenate(
        [gate_weight, jnp.zeros((gate_weight.shape[0], gap), BF16), up_weight], axis=1
    )
    whole = lax.all_gather(stacked, "dp", axis=0, tiled=True)

    video_rows = patch_count // 4
    seq_count = video_rows + audio.shape[0]
    capacity = 2 * seq_count // owner_count
    sent_lengths = span_lengths[owner]
    starts = jnp.cumsum(sent_lengths) - sent_lengths
    slot_index = jnp.arange(capacity, dtype=jnp.int32)
    row_of_slot = jnp.where(
        slot_index[None, :] < sent_lengths[:, None], starts[:, None] + slot_index[None, :], -1
    ).reshape(-1)
    row = jnp.arange(seq_count, dtype=jnp.int32)
    select = (row_of_slot[:, None] == row[None, video_rows:]).astype(BF16)
    from_audio = jnp.dot(select, audio, preferred_element_type=F32).astype(BF16)
    slots = owner_count * capacity
    width = audio.shape[1]
    operands = [*contexts[: n - 1], own_head, above, below, other, patches]
    sofar = call(
        functools.partial(project_kernel, n),
        jax.ShapeDtypeStruct((patch_count, d_vit), F32),
        [hbm] * len(operands),
        2 * patch_count * d_vit * d_vit,
        scratch=[pltpu.VMEM(a.shape, BF16) for a in operands]
        + [
            pltpu.VMEM(((n - 1) * group, patch_count), BF16),
            pltpu.VMEM(((n - 1) * group, d_vit), BF16),
            pltpu.SemaphoreType.DMA((len(operands),)),
        ],
        mib=62,
    )(*operands)
    outgoing = call(
        merge_kernel,
        jax.ShapeDtypeStruct((slots, width), BF16),
        [vmem] * 5 + [hbm, vmem, hbm],
        2 * patch_count * d_vit * width,
        scratch=[
            pltpu.VMEM((group, patch_count), BF16),
            pltpu.VMEM((group, d_vit), BF16),
            pltpu.VMEM((d_vit // 128, patch_count, 128), F32),
            pltpu.VMEM(merger_weight.shape[::-1], BF16),
            pltpu.VMEM((slots, width), BF16),
            pltpu.SemaphoreType.DMA((2,)),
        ],
        mib=62,
    )(
        contexts[n - 1],
        tall[-1],
        last,
        sofar,
        merge_gain[None, :],
        merger_weight.T,
        row_of_slot[:, None],
        from_audio,
    )
    incoming = lax.all_to_all(
        outgoing.reshape(owner_count, capacity, width), "dp", split_axis=0, concat_axis=0, tiled=True
    ).reshape(slots, width)
    taken_lengths = span_lengths[:, owner]
    arrival = span_time[owner]
    earlier = arrival[:, None] < arrival[None, :]
    offsets = jnp.sum(jnp.where(earlier, taken_lengths[:, None], 0), axis=0)
    target = jnp.where(
        slot_index[None, :] < taken_lengths[:, None], offsets[:, None] + slot_index[None, :], -1
    ).reshape(1, -1)
    sequence = call(
        pick_kernel,
        jax.ShapeDtypeStruct((seq_count, width), BF16),
        [vmem] * 2,
        2 * slots * seq_count * width,
        mib=16,
    )(target, incoming)

    down_turned, sequence = lax.optimization_barrier((down_weight.T, sequence))
    down_whole = lax.all_gather(down_turned, "dp", axis=0, tiled=True)

    features = n * width
    own_count = seq_count // n
    got = ring_blocks(sequence, "tensor")
    order = sorted(got)
    hidden, own_rows = call(
        functools.partial(gate_kernel, n, tuple(order), units),
        (
            jax.ShapeDtypeStruct((seq_count, units), BF16),
            jax.ShapeDtypeStruct((n, own_count, width), BF16),
        ),
        [smem] + [hbm] * n + [vmem, hbm],
        4 * seq_count * features * units,
        scratch=[
            pltpu.VMEM((n, seq_count, width), BF16),
            pltpu.VMEM((features, 2 * units + gap), BF16),
            pltpu.VMEM((seq_count, features), BF16),
            pltpu.SemaphoreType.DMA((2 * n,)),
        ],
        mib=62,
    )(plane.reshape(1), *[got[k] for k in order], llm_gain.reshape(n, 1, width), whole)
    terms = call(
        down_kernel,
        jax.ShapeDtypeStruct((seq_count, features), BF16),
        [vmem, hbm],
        2 * seq_count * features * units,
        scratch=[
            pltpu.VMEM((features, units), BF16),
            pltpu.VMEM((seq_count, features), BF16),
            pltpu.SemaphoreType.DMA((2 * (features // 256),)),
        ],
        mib=62,
        out_space=HBM,
    )(hidden, down_whole)
    summed = lax.psum_scatter(terms, "tensor", scatter_dimension=0, tiled=True).astype(F32)
    own_rows = jnp.moveaxis(own_rows, 0, 1).reshape(own_count, features)
    return (own_rows.astype(F32) + summed).astype(BF16)


def solution(mesh):
    return jax.shard_map(
        body,
        mesh=mesh,
        in_specs=(
            P("dp", None),
            P("dp", None),
            P(),
            P(None, None, "tensor"),
            P("tensor", None),
            P(),
            P(None, "tensor"),
            P("dp", "tensor"),
            P(),
            P(),
            P(),
            P("dp", "tensor"),
            P("dp", "tensor"),
            P("tensor", "dp"),
        ),
        out_specs=P(("dp", "tensor"), None),
        check_vma=False,
    )
```

```python
import functools
import math

import jax
import jax.numpy as jnp
from jax import lax
from jax.experimental import pallas as pl
from jax.experimental.pallas import tpu as pltpu
from jax.sharding import PartitionSpec as P

HEAD_VIT = 80
EPSILON = 1e-06
VMEM = pltpu.MemorySpace.VMEM
SMEM = pltpu.MemorySpace.SMEM
HBM = pltpu.MemorySpace.HBM
BF16 = jnp.bfloat16
F32 = jnp.float32


def shifted(axis, step):
    n = lax.axis_size(axis)
    return [(i, (i + step) % n) for i in range(n)]


def ring_blocks(x, axis):
    n = lax.axis_size(axis)
    blocks = {0: x}
    a = b = x
    for k in range(1, n // 2 + 1):
        a = lax.ppermute(a, axis, shifted(axis, 1))
        blocks[-k] = a
        if k < n - n // 2:
            b = lax.ppermute(b, axis, shifted(axis, -1))
            blocks[k] = b
    return blocks


def turned_dot(left, right):
    return lax.dot_general(left, right, (((1,), (1,)), ((), ())), preferred_element_type=F32)


def inverse_rms(wide):
    return lax.rsqrt(jnp.mean(wide * wide, axis=-1, keepdims=True) + EPSILON)


def vision_kernel(core_ref, patches_ref, column_ref, row_ref, gain_ref, weight_ref, out_ref):
    wide = patches_ref[...].astype(F32)
    normed = (wide * inverse_rms(wide) * gain_ref[...]).astype(BF16)
    query, keys, values = (
        turned_dot(normed, weight_ref[k]).astype(BF16) for k in range(3)
    )
    same = column_ref[...] == row_ref[...]
    for head in range(2):
        part = slice(head * HEAD_VIT, (head + 1) * HEAD_VIT)
        scores = turned_dot(query[:, part], keys[:, part])
        scores = jnp.where(same, scores * (1.0 / math.sqrt(HEAD_VIT)), -1e30)
        weights = jnp.exp(scores - jnp.max(scores, axis=-1, keepdims=True))
        probs = (weights / jnp.sum(weights, axis=-1, keepdims=True)).astype(BF16)
        context = lax.dot_general(
            values[:, part], probs, (((0,), (1,)), ((), ())), preferred_element_type=F32
        )
        place = pl.multiple_of(lax.rem(core_ref[0] + head, 2) * HEAD_VIT, 16)
        out_ref[pl.ds(place, HEAD_VIT), :] = context.astype(BF16)


def lay(into, at, wide):
    rows, columns = wide.shape
    for j in range(columns // 128):
        into[pl.ds(at + j * rows, rows), :] = wide[:, pl.ds(j * 128, 128)]


def spread(into, at, tall, start, rows):
    for j in range(into.shape[1] // 128):
        into[pl.ds(at, rows), pl.ds(j * 128, 128)] = tall[pl.ds(start + j * rows, rows), :]


def pack_kernel(context_ref, above_ref, below_ref, up_ref, down_ref):
    split = context_ref.size // 128
    for out_ref, block_ref in ((up_ref, above_ref), (down_ref, below_ref)):
        lay(out_ref, 0, context_ref)
        lay(out_ref, split, block_ref)


def stack_kernel(wide_count, *refs):
    blocks, out_ref = refs[:-1], refs[-1]
    rows = out_ref.shape[1]
    for k, ref in enumerate(blocks):
        if k < wide_count:
            lay(out_ref.at[k], 0, ref)
        else:
            out_ref[k] = ref[pl.ds(ref.shape[0] - rows, rows), :]


def project_kernel(n, *refs):
    count = n + 4
    sources, out_ref, sems = refs[:count], refs[count], refs[-1]
    places, (context, weight) = refs[count + 1 : 2 * count + 1], refs[2 * count + 1 : 2 * count + 3]
    fetch = [
        pltpu.make_async_copy(source, place, sems.at[k])
        for k, (source, place) in enumerate(zip(sources, places))
    ]
    for copy in fetch:
        copy.start()
    payloads, wide, (other, patches) = places[: n - 1], places[n - 1 : n + 2], places[n + 2 :]
    group = 2 * HEAD_VIT
    split = group * context.shape[1] // 128
    for k in range(n - 1):
        fetch[k].wait()
        spread(context, k * group, payloads[k], 0, group)
    for k in range(3):
        fetch[n - 1 + k].wait()
        weight[pl.ds(k * group, HEAD_VIT), :] = wide[k][...]
    for k in range(3, n - 1):
        spread(weight, k * group, payloads[k - 2], split, HEAD_VIT)
    turned = context[...].T
    fetch[n + 2].wait()
    for k in range(n - 1):
        spread(weight, k * group + HEAD_VIT, other.at[k], 0, HEAD_VIT)
    fetch[n + 3].wait()

    @pl.loop(0, out_ref.shape[1] // 256)
    def _(j):
        columns = pl.ds(pl.multiple_of(j * 256, 256), 256)
        attended = jnp.dot(turned, weight[:, columns], preferred_element_type=F32)
        out_ref[:, columns] = patches[:, columns].astype(F32) + attended


def merge_kernel(*refs):
    context_ref, mine_ref, last_ref, sofar_ref, gain_ref, merger_hbm, slot_ref, audio_hbm, out_ref = refs[:9]
    context, weight, normed, merger, audio, sems = refs[9:]
    fetch = [
        pltpu.make_async_copy(merger_hbm, merger, sems.at[0]),
        pltpu.make_async_copy(audio_hbm, audio, sems.at[1]),
    ]
    for copy in fetch:
        copy.start()
    rows, d_vit = sofar_ref.shape
    group = 2 * HEAD_VIT
    split = group * rows // 128
    spread(context, 0, context_ref, 0, group)
    spread(weight, 0, mine_ref, split, HEAD_VIT)
    spread(weight, HEAD_VIT, last_ref, split, HEAD_VIT)
    turned = context[...].T
    lanes = 128
    squares = jnp.zeros((rows, 1), F32)
    for j in range(d_vit // 256):
        columns = pl.ds(j * 256, 256)
        attended = jnp.dot(turned, weight[:, columns], preferred_element_type=F32)
        wide = (sofar_ref[:, columns] + attended).astype(BF16).astype(F32)
        squares += jnp.sum(wide * wide, axis=-1, keepdims=True)
        normed[2 * j] = wide[:, :lanes]
        normed[2 * j + 1] = wide[:, lanes:]
    scale = lax.rsqrt(squares / d_vit + EPSILON)
    for j in range(d_vit // lanes):
        normed[j] = normed[j] * scale * gain_ref[:, pl.ds(j * lanes, lanes)]

    fetch[0].wait()
    video = jnp.zeros((rows // 4, merger.shape[0]), F32)
    for j in range(4):
        part = [normed[k, pl.ds(j, rows // 4, stride=4), :] for k in range(d_vit // lanes)]
        part = jnp.concatenate(part, axis=1).astype(BF16)
        video += turned_dot(part, merger[:, pl.ds(j * d_vit, d_vit)])
    video = video.astype(BF16)
    index = lax.broadcasted_iota(jnp.int32, (slot_ref.shape[0], rows // 4), 1)
    select = (slot_ref[...] == index).astype(F32).astype(BF16)
    placed = jnp.dot(select, video, preferred_element_type=F32)
    fetch[1].wait()
    out_ref[...] = (placed + audio[...].astype(F32)).astype(BF16)


def pick_kernel(target_ref, incoming_ref, out_ref):
    row = lax.broadcasted_iota(jnp.int32, (out_ref.shape[0], incoming_ref.shape[0]), 0)
    pick = (row == target_ref[...]).astype(F32).astype(BF16)
    out_ref[...] = jnp.dot(pick, incoming_ref[...], preferred_element_type=F32).astype(BF16)


def rows_fetch(place, shifts, n, whole_hbm, whole, sems):
    chunk = whole.shape[0] // len(shifts)
    fetch = []
    for j, shift in enumerate(shifts):
        at = lax.rem(place + shift + n, n)
        source = whole_hbm.at[pl.ds(pl.multiple_of(at * chunk, 16), chunk), :]
        fetch.append(pltpu.make_async_copy(source, whole.at[pl.ds(j * chunk, chunk), :], sems.at[j]))
    return fetch


def scaled_blocks(blocks, gains, scaled, squares):
    chunk = blocks[0].shape[1]
    for j, block in enumerate(blocks):
        wide = block[...].astype(F32)
        squares += jnp.sum(wide * wide, axis=-1, keepdims=True)
        scaled[:, pl.ds(j * chunk, chunk)] = (wide * gains[j]).astype(BF16)
    return squares


def early_kernel(shifts, place_ref, *refs):
    count = len(shifts)
    blocks, gain_ref, whole_hbm, sums_ref, squares_ref, scaled, whole, sems = refs[:count], *refs[count:]
    n = gain_ref.shape[0]
    fetch = rows_fetch(place_ref[0], shifts, n, whole_hbm, whole, sems)
    for copy in fetch:
        copy.start()
    gains = [gain_ref[lax.rem(place_ref[0] + shift + n, n)] for shift in shifts]
    zero = jnp.zeros((blocks[0].shape[0], 1), F32)
    squares_ref[...] = scaled_blocks(blocks, gains, scaled, zero)
    for copy in fetch:
        copy.wait()
    tile = 256
    width = sums_ref.shape[1]

    def step(start, size):
        sums_ref[:, pl.ds(start, size)] = jnp.dot(
            scaled[...], whole[:, pl.ds(start, size)], preferred_element_type=F32
        )

    @pl.loop(0, width // tile)
    def _(j):
        step(pl.multiple_of(j * tile, tile), tile)

    if width % tile:
        step(width // tile * tile, width % tile)


def late_kernel(shifts, early, units, place_ref, *refs):
    n = len(shifts)
    blocks, gain_ref, whole_hbm, sums_ref, squares_ref, hidden_ref, own_ref = refs[:n], *refs[n : n + 6]
    scaled, whole, sems = refs[n + 6 :]
    fetch = rows_fetch(place_ref[0], shifts[early:], n, whole_hbm, whole, sems)
    for copy in fetch:
        copy.start()
    places = [lax.rem(place_ref[0] + shift + n, n) for shift in shifts]
    gains = [gain_ref[at] for at in places[early:]]
    squares = scaled_blocks(blocks[early:], gains, scaled, squares_ref[...])
    scale = lax.rsqrt(squares / whole_hbm.shape[0] + EPSILON)
    own = own_ref.shape[1]
    first = pl.multiple_of(place_ref[0] * own, own)
    for at, block in zip(places, blocks):
        own_ref[at] = block[pl.ds(first, own), :]
    for copy in fetch:
        copy.wait()
    apart, tile = whole.shape[1] - units, 256

    def step(start, size):
        gate, upward = (
            scale
            * (
                sums_ref[:, pl.ds(at, size)]
                + jnp.dot(scaled[...], whole[:, pl.ds(at, size)], preferred_element_type=F32)
            )
            for at in (start, apart + start)
        )
        value = gate * (1.0 / (1.0 + jnp.exp(-gate))) * upward
        hidden_ref[:, pl.ds(start, size)] = value.astype(BF16)

    @pl.loop(0, units // tile)
    def _(j):
        step(pl.multiple_of(j * tile, tile), tile)

    step(units // tile * tile, units % tile)


def down_kernel(tile, hidden_ref, weight_hbm, out_hbm, weight, out, sems):
    tiles = weight.shape[0] // tile

    def here(j):
        return pl.ds(pl.multiple_of(j * tile, tile), tile)

    def part(j):
        return pltpu.make_async_copy(weight_hbm.at[here(j), :], weight.at[here(j), :], sems.at[j])

    def result(j):
        return pltpu.make_async_copy(out.at[:, here(j)], out_hbm.at[:, here(j)], sems.at[tiles + j])

    @pl.loop(0, tiles)
    def _(j):
        part(j).start()

    @pl.loop(0, tiles)
    def _(j):
        part(j).wait()
        out[:, here(j)] = turned_dot(hidden_ref[...], weight[here(j), :]).astype(BF16)
        result(j).start()

    @pl.loop(0, tiles)
    def _(j):
        result(j).wait()


def call(kernel, out_shape, specs, flops, scratch=(), mib=16, out_space=VMEM):
    def run(*args):
        moved = sum(a.size * a.dtype.itemsize for a in args)
        return pl.pallas_call(
            kernel,
            out_shape=out_shape,
            in_specs=specs,
            out_specs=jax.tree.map(lambda _: pl.BlockSpec(memory_space=out_space), out_shape),
            scratch_shapes=scratch,
            compiler_params=pltpu.CompilerParams(vmem_limit_bytes=mib << 20),
            cost_estimate=pl.CostEstimate(flops=flops, bytes_accessed=moved, transcendentals=0),
        )(*args)

    return run


def body(
    patches,
    window_ids,
    vit_gain,
    qkv_weight,
    out_weight,
    merge_gain,
    merger_weight,
    audio,
    span_lengths,
    span_time,
    llm_gain,
    gate_weight,
    up_weight,
    down_weight,
):
    patch_count, d_vit = patches.shape
    n = lax.axis_size("tensor")
    owner_count = lax.axis_size("dp")
    owner = lax.axis_index("dp")
    plane = lax.axis_index("tensor")
    core = lax.rem(owner, 2)
    units = gate_weight.shape[1]
    vmem = pl.BlockSpec(memory_space=VMEM)
    smem = pl.BlockSpec(memory_space=SMEM)
    hbm = pl.BlockSpec(memory_space=HBM)

    windows = window_ids[0]
    context = call(
        vision_kernel,
        jax.ShapeDtypeStruct((2 * HEAD_VIT, patch_count), BF16),
        [smem] + [vmem] * 5,
        2 * patch_count * (3 * d_vit * 160 + 4 * patch_count * HEAD_VIT),
    )(
        core.reshape(1),
        patches,
        windows[:, None],
        windows[None, :],
        vit_gain[None, :],
        jnp.swapaxes(qkv_weight, 1, 2),
    )

    group = 2 * HEAD_VIT
    own_head = lax.dynamic_slice_in_dim(out_weight, core * HEAD_VIT, HEAD_VIT, 0)
    above = lax.ppermute(own_head, "tensor", shifted("tensor", 1))
    below = lax.ppermute(own_head, "tensor", shifted("tensor", -1))
    split, block_rows = group * patch_count // 128, HEAD_VIT * d_vit // 128
    payload = jax.ShapeDtypeStruct((split + block_rows, 128), BF16)
    up, down = call(pack_kernel, (payload, payload), [vmem] * 3, 0)(context, above, below)
    ups, downs = [up], [down]
    for k in range(1, n // 2):
        ups.append(lax.ppermute(ups[-1], "tensor", shifted("tensor", 1)))
        away = downs[-1] if k < n // 2 - 1 else downs[-1][:split]
        downs.append(lax.ppermute(away, "tensor", shifted("tensor", -1)))
    ups.append(lax.ppermute(ups[-1][:split], "tensor", shifted("tensor", 1)))
    contexts = [up]
    tall = []
    for k in range(1, n // 2 + 1):
        contexts.append(ups[k])
        if k < n // 2:
            contexts.append(downs[k])
            tall.append(ups[k])
        if k < n // 2 - 1:
            tall.append(downs[k])
    swap = [(i, i ^ 1) for i in range(owner_count)]
    laid = call(
        functools.partial(stack_kernel, 3),
        jax.ShapeDtypeStruct((n - 1, block_rows, 128), BF16),
        [vmem] * (n - 1),
        0,
    )(own_head, above, below, *tall[:-1])
    other = lax.ppermute(laid, "dp", swap)
    last = lax.ppermute(tall[-1], "dp", swap)

    gap = -units % 128
    stacked = jnp.concatenate(
        [gate_weight, jnp.zeros((gate_weight.shape[0], gap), BF16), up_weight], axis=1
    )
    whole = lax.all_gather(stacked, "dp", axis=0, tiled=True)

    video_rows = patch_count // 4
    seq_count = video_rows + audio.shape[0]
    capacity = 2 * seq_count // owner_count
    sent_lengths = span_lengths[owner]
    starts = jnp.cumsum(sent_lengths) - sent_lengths
    slot_index = jnp.arange(capacity, dtype=jnp.int32)
    row_of_slot = jnp.where(
        slot_index[None, :] < sent_lengths[:, None], starts[:, None] + slot_index[None, :], -1
    ).reshape(-1)
    row = jnp.arange(seq_count, dtype=jnp.int32)
    select = (row_of_slot[:, None] == row[None, video_rows:]).astype(BF16)
    from_audio = jnp.dot(select, audio, preferred_element_type=F32).astype(BF16)
    slots = owner_count * capacity
    width = audio.shape[1]
    operands = [*contexts[: n - 1], own_head, above, below, other, patches]
    sofar = call(
        functools.partial(project_kernel, n),
        jax.ShapeDtypeStruct((patch_count, d_vit), F32),
        [hbm] * len(operands),
        2 * patch_count * d_vit * d_vit,
        scratch=[pltpu.VMEM(a.shape, BF16) for a in operands]
        + [
            pltpu.VMEM(((n - 1) * group, patch_count), BF16),
            pltpu.VMEM(((n - 1) * group, d_vit), BF16),
            pltpu.SemaphoreType.DMA((len(operands),)),
        ],
        mib=62,
    )(*operands)
    outgoing = call(
        merge_kernel,
        jax.ShapeDtypeStruct((slots, width), BF16),
        [vmem] * 5 + [hbm, vmem, hbm],
        2 * patch_count * d_vit * width,
        scratch=[
            pltpu.VMEM((group, patch_count), BF16),
            pltpu.VMEM((group, d_vit), BF16),
            pltpu.VMEM((d_vit // 128, patch_count, 128), F32),
            pltpu.VMEM(merger_weight.shape[::-1], BF16),
            pltpu.VMEM((slots, width), BF16),
            pltpu.SemaphoreType.DMA((2,)),
        ],
        mib=62,
    )(
        contexts[n - 1],
        tall[-1],
        last,
        sofar,
        merge_gain[None, :],
        merger_weight.T,
        row_of_slot[:, None],
        from_audio,
    )
    down_turned, outgoing = lax.optimization_barrier((down_weight.T, outgoing))
    down_whole = lax.all_gather(down_turned, "dp", axis=0, tiled=True)
    incoming = lax.all_to_all(
        outgoing.reshape(owner_count, capacity, width), "dp", split_axis=0, concat_axis=0, tiled=True
    ).reshape(slots, width)
    taken_lengths = span_lengths[:, owner]
    arrival = span_time[owner]
    earlier = arrival[:, None] < arrival[None, :]
    offsets = jnp.sum(jnp.where(earlier, taken_lengths[:, None], 0), axis=0)
    target = jnp.where(
        slot_index[None, :] < taken_lengths[:, None], offsets[:, None] + slot_index[None, :], -1
    ).reshape(1, -1)
    sequence = call(
        pick_kernel,
        jax.ShapeDtypeStruct((seq_count, width), BF16),
        [vmem] * 2,
        2 * slots * seq_count * width,
        mib=16,
    )(target, incoming)

    features = n * width
    own_count = seq_count // n
    shifts = [0]
    for k in range(1, n // 2):
        shifts += [-k, k]
    shifts.append(-(n // 2))
    early = 5
    here = plane.reshape(1)
    padded = 2 * units + gap
    gains = llm_gain.reshape(n, 1, width)
    blocks = [sequence]
    a = b = sequence
    for k in range(1, n // 2 + 1):
        a = lax.ppermute(a, "tensor", shifted("tensor", 1))
        if k < n // 2:
            b = lax.ppermute(b, "tensor", shifted("tensor", -1))
        if k == 3:
            sums, squares = call(
                functools.partial(early_kernel, shifts[:early]),
                (
                    jax.ShapeDtypeStruct((seq_count, padded), F32),
                    jax.ShapeDtypeStruct((seq_count, 1), F32),
                ),
                [smem] + [vmem] * (early + 1) + [hbm],
                4 * seq_count * early * width * units,
                scratch=[
                    pltpu.VMEM((seq_count, early * width), BF16),
                    pltpu.VMEM((early * width, padded), BF16),
                    pltpu.SemaphoreType.DMA((early,)),
                ],
                mib=48,
            )(here, *blocks, gains, whole)
            a, b, sums = lax.optimization_barrier((a, b, sums))
        blocks.append(a)
        if k < n // 2:
            blocks.append(b)
    hidden, own_rows = call(
        functools.partial(late_kernel, shifts, early, units),
        (
            jax.ShapeDtypeStruct((seq_count, units), BF16),
            jax.ShapeDtypeStruct((n, own_count, width), BF16),
        ),
        [smem] + [vmem] * (n + 1) + [hbm] + [vmem] * 2,
        4 * seq_count * (n - early) * width * units,
        scratch=[
            pltpu.VMEM((seq_count, (n - early) * width), BF16),
            pltpu.VMEM(((n - early) * width, padded), BF16),
            pltpu.SemaphoreType.DMA((n - early,)),
        ],
        mib=48,
    )(here, *blocks, gains, whole, sums, squares)
    down_tile = 512
    terms = call(
        functools.partial(down_kernel, down_tile),
        jax.ShapeDtypeStruct((seq_count, features), BF16),
        [vmem, hbm],
        2 * seq_count * features * units,
        scratch=[
            pltpu.VMEM((features, units), BF16),
            pltpu.VMEM((seq_count, features), BF16),
            pltpu.SemaphoreType.DMA((2 * (features // down_tile),)),
        ],
        mib=62,
        out_space=HBM,
    )(hidden, down_whole)
    summed = lax.psum_scatter(terms, "tensor", scatter_dimension=0, tiled=True).astype(F32)
    own_rows = jnp.moveaxis(own_rows, 0, 1).reshape(own_count, features)
    return (own_rows.astype(F32) + summed).astype(BF16)


def solution(mesh):
    return jax.shard_map(
        body,
        mesh=mesh,
        in_specs=(
            P("dp", None),
            P("dp", None),
            P(),
            P(None, None, "tensor"),
            P("tensor", None),
            P(),
            P(None, "tensor"),
            P("dp", "tensor"),
            P(),
            P(),
            P(),
            P("dp", "tensor"),
            P("dp", "tensor"),
            P("tensor", "dp"),
        ),
        out_specs=P(("dp", "tensor"), None),
        check_vma=False,
    )
```

```python
import functools
import math

import jax
import jax.numpy as jnp
from jax import lax
from jax.experimental import pallas as pl
from jax.experimental.pallas import tpu as pltpu
from jax.sharding import PartitionSpec as P

HEAD_VIT = 80
EPSILON = 1e-06
VMEM = pltpu.MemorySpace.VMEM
SMEM = pltpu.MemorySpace.SMEM
HBM = pltpu.MemorySpace.HBM
BF16 = jnp.bfloat16
F32 = jnp.float32


def shifted(axis, step):
    n = lax.axis_size(axis)
    return [(i, (i + step) % n) for i in range(n)]


def ring_blocks(x, axis):
    n = lax.axis_size(axis)
    blocks = {0: x}
    a = b = x
    for k in range(1, n // 2 + 1):
        a = lax.ppermute(a, axis, shifted(axis, 1))
        blocks[-k] = a
        if k < n - n // 2:
            b = lax.ppermute(b, axis, shifted(axis, -1))
            blocks[k] = b
    return blocks


def turned_dot(left, right):
    return lax.dot_general(left, right, (((1,), (1,)), ((), ())), preferred_element_type=F32)


def inverse_rms(wide):
    return lax.rsqrt(jnp.mean(wide * wide, axis=-1, keepdims=True) + EPSILON)


def vision_kernel(core_ref, patches_ref, column_ref, row_ref, gain_ref, weight_ref, out_ref):
    wide = patches_ref[...].astype(F32)
    normed = (wide * inverse_rms(wide) * gain_ref[...]).astype(BF16)
    query, keys, values = (
        turned_dot(normed, weight_ref[k]).astype(BF16) for k in range(3)
    )
    same = column_ref[...] == row_ref[...]
    for head in range(2):
        part = slice(head * HEAD_VIT, (head + 1) * HEAD_VIT)
        scores = turned_dot(query[:, part], keys[:, part])
        scores = jnp.where(same, scores * (1.0 / math.sqrt(HEAD_VIT)), -1e30)
        weights = jnp.exp(scores - jnp.max(scores, axis=-1, keepdims=True))
        probs = (weights / jnp.sum(weights, axis=-1, keepdims=True)).astype(BF16)
        context = lax.dot_general(
            values[:, part], probs, (((0,), (1,)), ((), ())), preferred_element_type=F32
        )
        place = pl.multiple_of(lax.rem(core_ref[0] + head, 2) * HEAD_VIT, 16)
        out_ref[pl.ds(place, HEAD_VIT), :] = context.astype(BF16)


def lay(into, at, wide):
    rows, columns = wide.shape
    for j in range(columns // 128):
        into[pl.ds(at + j * rows, rows), :] = wide[:, pl.ds(j * 128, 128)]


def spread(into, at, tall, start, rows):
    for j in range(into.shape[1] // 128):
        into[pl.ds(at, rows), pl.ds(j * 128, 128)] = tall[pl.ds(start + j * rows, rows), :]


def pack_kernel(context_ref, above_ref, below_ref, up_ref, down_ref):
    split = context_ref.size // 128
    for out_ref, block_ref in ((up_ref, above_ref), (down_ref, below_ref)):
        lay(out_ref, 0, context_ref)
        lay(out_ref, split, block_ref)


def stack_kernel(wide_count, *refs):
    blocks, out_ref = refs[:-1], refs[-1]
    rows = out_ref.shape[1]
    for k, ref in enumerate(blocks):
        if k < wide_count:
            lay(out_ref.at[k], 0, ref)
        else:
            out_ref[k] = ref[pl.ds(ref.shape[0] - rows, rows), :]


def project_kernel(n, *refs):
    count = n + 4
    sources, out_ref, sems = refs[:count], refs[count], refs[-1]
    places, (context, weight) = refs[count + 1 : 2 * count + 1], refs[2 * count + 1 : 2 * count + 3]
    fetch = [
        pltpu.make_async_copy(source, place, sems.at[k])
        for k, (source, place) in enumerate(zip(sources, places))
    ]
    for copy in fetch:
        copy.start()
    payloads, wide, (other, patches) = places[: n - 1], places[n - 1 : n + 2], places[n + 2 :]
    group = 2 * HEAD_VIT
    split = group * context.shape[1] // 128
    for k in range(n - 1):
        fetch[k].wait()
        spread(context, k * group, payloads[k], 0, group)
    for k in range(3):
        fetch[n - 1 + k].wait()
        weight[pl.ds(k * group, HEAD_VIT), :] = wide[k][...]
    for k in range(3, n - 1):
        spread(weight, k * group, payloads[k - 2], split, HEAD_VIT)
    turned = context[...].T
    fetch[n + 2].wait()
    for k in range(n - 1):
        spread(weight, k * group + HEAD_VIT, other.at[k], 0, HEAD_VIT)
    fetch[n + 3].wait()

    @pl.loop(0, out_ref.shape[1] // 256)
    def _(j):
        columns = pl.ds(pl.multiple_of(j * 256, 256), 256)
        attended = jnp.dot(turned, weight[:, columns], preferred_element_type=F32)
        out_ref[:, columns] = patches[:, columns].astype(F32) + attended


def merge_kernel(*refs):
    context_ref, mine_ref, last_ref, sofar_ref, gain_ref, merger_hbm, slot_ref, audio_hbm, out_ref = refs[:9]
    context, weight, normed, merger, audio, sems = refs[9:]
    fetch = [
        pltpu.make_async_copy(merger_hbm, merger, sems.at[0]),
        pltpu.make_async_copy(audio_hbm, audio, sems.at[1]),
    ]
    for copy in fetch:
        copy.start()
    rows, d_vit = sofar_ref.shape
    group = 2 * HEAD_VIT
    split = group * rows // 128
    spread(context, 0, context_ref, 0, group)
    spread(weight, 0, mine_ref, split, HEAD_VIT)
    spread(weight, HEAD_VIT, last_ref, split, HEAD_VIT)
    turned = context[...].T
    lanes = 128
    squares = jnp.zeros((rows, 1), F32)
    for j in range(d_vit // 256):
        columns = pl.ds(j * 256, 256)
        attended = jnp.dot(turned, weight[:, columns], preferred_element_type=F32)
        wide = (sofar_ref[:, columns] + attended).astype(BF16).astype(F32)
        squares += jnp.sum(wide * wide, axis=-1, keepdims=True)
        normed[2 * j] = wide[:, :lanes]
        normed[2 * j + 1] = wide[:, lanes:]
    scale = lax.rsqrt(squares / d_vit + EPSILON)
    for j in range(d_vit // lanes):
        normed[j] = normed[j] * scale * gain_ref[:, pl.ds(j * lanes, lanes)]

    fetch[0].wait()
    video = jnp.zeros((rows // 4, merger.shape[0]), F32)
    for j in range(4):
        part = [normed[k, pl.ds(j, rows // 4, stride=4), :] for k in range(d_vit // lanes)]
        part = jnp.concatenate(part, axis=1).astype(BF16)
        video += turned_dot(part, merger[:, pl.ds(j * d_vit, d_vit)])
    video = video.astype(BF16)
    index = lax.broadcasted_iota(jnp.int32, (slot_ref.shape[0], rows // 4), 1)
    select = (slot_ref[...] == index).astype(F32).astype(BF16)
    placed = jnp.dot(select, video, preferred_element_type=F32)
    fetch[1].wait()
    out_ref[...] = (placed + audio[...].astype(F32)).astype(BF16)


def pick_kernel(target_ref, incoming_ref, out_ref):
    row = lax.broadcasted_iota(jnp.int32, (out_ref.shape[0], incoming_ref.shape[0]), 0)
    pick = (row == target_ref[...]).astype(F32).astype(BF16)
    out_ref[...] = jnp.dot(pick, incoming_ref[...], preferred_element_type=F32).astype(BF16)


def rows_fetch(place, shifts, n, whole_hbm, whole, sems):
    chunk = whole.shape[0] // len(shifts)
    fetch = []
    for j, shift in enumerate(shifts):
        at = lax.rem(place + shift + n, n)
        source = whole_hbm.at[pl.ds(pl.multiple_of(at * chunk, 16), chunk), :]
        fetch.append(pltpu.make_async_copy(source, whole.at[pl.ds(j * chunk, chunk), :], sems.at[j]))
    return fetch


def scaled_blocks(blocks, gains, scaled, squares):
    chunk = blocks[0].shape[1]
    for j, block in enumerate(blocks):
        wide = block[...].astype(F32)
        squares += jnp.sum(wide * wide, axis=-1, keepdims=True)
        scaled[:, pl.ds(j * chunk, chunk)] = (wide * gains[j]).astype(BF16)
    return squares


def early_kernel(shifts, place_ref, *refs):
    count = len(shifts)
    blocks, gain_ref, whole_hbm, sums_hbm, squares_ref = refs[:count], *refs[count : count + 4]
    scaled, whole, sums, sems = refs[count + 4 :]
    n = gain_ref.shape[0]
    fetch = rows_fetch(place_ref[0], shifts, n, whole_hbm, whole, sems)
    for copy in fetch:
        copy.start()
    gains = [gain_ref[lax.rem(place_ref[0] + shift + n, n)] for shift in shifts]
    zero = jnp.zeros((blocks[0].shape[0], 1), F32)
    squares_ref[...] = scaled_blocks(blocks, gains, scaled, zero)
    for copy in fetch:
        copy.wait()
    width = sums.shape[1]
    tile = 256
    full = width // tile

    def result(columns, j):
        return pltpu.make_async_copy(sums.at[:, columns], sums_hbm.at[:, columns], sems.at[count + j])

    def step(start, size, j):
        columns = pl.ds(start, size)
        sums[:, columns] = jnp.dot(scaled[...], whole[:, columns], preferred_element_type=F32)

    @pl.loop(0, full)
    def _(j):
        start = pl.multiple_of(j * tile, tile)
        step(start, tile, j)
        result(pl.ds(start, tile), j).start()

    rest = result(pl.ds(full * tile, width - full * tile), full)
    step(full * tile, width - full * tile, full)
    rest.start()

    @pl.loop(0, full)
    def _(j):
        result(pl.ds(pl.multiple_of(j * tile, tile), tile), j).wait()

    rest.wait()


def late_kernel(shifts, early, units, place_ref, *refs):
    n = len(shifts)
    blocks, gain_ref, whole_hbm, sums_hbm, squares_ref, hidden_ref, own_ref = refs[:n], *refs[n : n + 6]
    scaled, whole, sums, sems = refs[n + 6 :]
    fetch = rows_fetch(place_ref[0], shifts[early:], n, whole_hbm, whole, sems)
    for copy in fetch:
        copy.start()
    bring = pltpu.make_async_copy(sums_hbm, sums, sems.at[n - early])
    bring.start()
    places = [lax.rem(place_ref[0] + shift + n, n) for shift in shifts]
    gains = [gain_ref[at] for at in places[early:]]
    squares = scaled_blocks(blocks[early:], gains, scaled, squares_ref[...])
    scale = lax.rsqrt(squares / whole_hbm.shape[0] + EPSILON)
    own = own_ref.shape[1]
    first = pl.multiple_of(place_ref[0] * own, own)
    for at, block in zip(places, blocks):
        own_ref[at] = block[pl.ds(first, own), :]
    for copy in fetch:
        copy.wait()
    apart, tile = whole.shape[1] - units, 256

    def product(at, size):
        return jnp.dot(scaled[...], whole[:, pl.ds(at, size)], preferred_element_type=F32)

    def finish(start, size, gate, upward):
        gate = scale * (sums[:, pl.ds(start, size)] + gate)
        upward = scale * (sums[:, pl.ds(apart + start, size)] + upward)
        value = gate * (1.0 / (1.0 + jnp.exp(-gate))) * upward
        hidden_ref[:, pl.ds(start, size)] = value.astype(BF16)

    bring.wait()

    @pl.loop(0, units // tile)
    def _(j):
        start = pl.multiple_of(j * tile, tile)
        finish(start, tile, product(start, tile), product(apart + start, tile))

    start, size = units // tile * tile, units % tile
    finish(start, size, product(start, size), product(apart + start, size))


def down_kernel(tile, n, hidden_ref, weight_hbm, *refs):
    outs_hbm, weight, outs, sems = refs[:2], refs[2], refs[3:5], refs[5]
    tiles = weight.shape[0] // tile
    run = hidden_ref.shape[0] // n

    def here(j):
        return pl.ds(pl.multiple_of(j * tile, tile), tile)

    def part(j):
        return pltpu.make_async_copy(weight_hbm.at[here(j), :], weight.at[here(j), :], sems.at[j])

    def result(j, k):
        place = sems.at[(k + 1) * tiles + j]
        return pltpu.make_async_copy(outs[k].at[:, here(j)], outs_hbm[k].at[:, here(j)], place)

    @pl.loop(0, tiles)
    def _(j):
        part(j).start()

    @pl.loop(0, tiles)
    def _(j):
        part(j).wait()
        value = turned_dot(hidden_ref[...], weight[here(j), :]).astype(BF16).reshape(n, run, tile)
        for k in range(2):
            half = value[:, k * run // 2 : (k + 1) * run // 2]
            outs[k][:, here(j)] = half.reshape(n * run // 2, tile)
            result(j, k).start()

    @pl.loop(0, tiles)
    def _(j):
        for k in range(2):
            result(j, k).wait()


def call(kernel, out_shape, specs, flops, scratch=(), mib=16, out_space=VMEM):
    def run(*args):
        moved = sum(a.size * a.dtype.itemsize for a in args)
        if isinstance(out_shape, tuple):
            spaces = out_space if isinstance(out_space, tuple) else (out_space,) * len(out_shape)
            outs = tuple(pl.BlockSpec(memory_space=space) for space in spaces)
        else:
            outs = pl.BlockSpec(memory_space=out_space)
        return pl.pallas_call(
            kernel,
            out_shape=out_shape,
            in_specs=specs,
            out_specs=outs,
            scratch_shapes=scratch,
            compiler_params=pltpu.CompilerParams(vmem_limit_bytes=mib << 20),
            cost_estimate=pl.CostEstimate(flops=flops, bytes_accessed=moved, transcendentals=0),
        )(*args)

    return run


def body(
    patches,
    window_ids,
    vit_gain,
    qkv_weight,
    out_weight,
    merge_gain,
    merger_weight,
    audio,
    span_lengths,
    span_time,
    llm_gain,
    gate_weight,
    up_weight,
    down_weight,
):
    patch_count, d_vit = patches.shape
    n = lax.axis_size("tensor")
    owner_count = lax.axis_size("dp")
    owner = lax.axis_index("dp")
    plane = lax.axis_index("tensor")
    core = lax.rem(owner, 2)
    units = gate_weight.shape[1]
    vmem = pl.BlockSpec(memory_space=VMEM)
    smem = pl.BlockSpec(memory_space=SMEM)
    hbm = pl.BlockSpec(memory_space=HBM)

    windows = window_ids[0]
    context = call(
        vision_kernel,
        jax.ShapeDtypeStruct((2 * HEAD_VIT, patch_count), BF16),
        [smem] + [vmem] * 5,
        2 * patch_count * (3 * d_vit * 160 + 4 * patch_count * HEAD_VIT),
    )(
        core.reshape(1),
        patches,
        windows[:, None],
        windows[None, :],
        vit_gain[None, :],
        jnp.swapaxes(qkv_weight, 1, 2),
    )

    video_rows = patch_count // 4
    seq_count = video_rows + audio.shape[0]
    capacity = 2 * seq_count // owner_count
    sent_lengths = span_lengths[owner]
    starts = jnp.cumsum(sent_lengths) - sent_lengths
    slot_index = jnp.arange(capacity, dtype=jnp.int32)
    row_of_slot = jnp.where(
        slot_index[None, :] < sent_lengths[:, None], starts[:, None] + slot_index[None, :], -1
    ).reshape(-1)
    row = jnp.arange(seq_count, dtype=jnp.int32)
    select = (row_of_slot[:, None] == row[None, video_rows:]).astype(BF16)
    from_audio = jnp.dot(select, audio, preferred_element_type=F32).astype(BF16)
    group = 2 * HEAD_VIT
    own_head = lax.dynamic_slice_in_dim(out_weight, core * HEAD_VIT, HEAD_VIT, 0)
    above = lax.ppermute(own_head, "tensor", shifted("tensor", 1))
    below = lax.ppermute(own_head, "tensor", shifted("tensor", -1))
    split, block_rows = group * patch_count // 128, HEAD_VIT * d_vit // 128
    payload = jax.ShapeDtypeStruct((split + block_rows, 128), BF16)
    up, down = call(pack_kernel, (payload, payload), [vmem] * 3, 0)(context, above, below)
    ups, downs = [up], [down]
    for k in range(1, n // 2):
        if k == n // 2 - 1:
            up, from_audio, slot_column = lax.optimization_barrier(
                (ups[-1], from_audio, row_of_slot[:, None])
            )
            ups[-1] = up
        ups.append(lax.ppermute(ups[-1], "tensor", shifted("tensor", 1)))
        away = downs[-1] if k < n // 2 - 1 else downs[-1][:split]
        downs.append(lax.ppermute(away, "tensor", shifted("tensor", -1)))
    ups.append(lax.ppermute(ups[-1][:split], "tensor", shifted("tensor", 1)))
    contexts = [ups[0]]
    tall = []
    for k in range(1, n // 2 + 1):
        contexts.append(ups[k])
        if k < n // 2:
            contexts.append(downs[k])
            tall.append(ups[k])
        if k < n // 2 - 1:
            tall.append(downs[k])
    swap = [(i, i ^ 1) for i in range(owner_count)]
    laid = call(
        functools.partial(stack_kernel, 3),
        jax.ShapeDtypeStruct((n - 1, block_rows, 128), BF16),
        [vmem] * (n - 1),
        0,
    )(own_head, above, below, *tall[:-1])
    other = lax.ppermute(laid, "dp", swap)
    last = lax.ppermute(tall[-1], "dp", swap)

    gap = -units % 128
    stacked = jnp.concatenate(
        [gate_weight, jnp.zeros((gate_weight.shape[0], gap), BF16), up_weight], axis=1
    )
    whole = lax.all_gather(stacked, "dp", axis=0, tiled=True)

    slots = owner_count * capacity
    width = audio.shape[1]
    operands = [*contexts[: n - 1], own_head, above, below, other, patches]
    sofar = call(
        functools.partial(project_kernel, n),
        jax.ShapeDtypeStruct((patch_count, d_vit), F32),
        [hbm] * len(operands),
        2 * patch_count * d_vit * d_vit,
        scratch=[pltpu.VMEM(a.shape, BF16) for a in operands]
        + [
            pltpu.VMEM(((n - 1) * group, patch_count), BF16),
            pltpu.VMEM(((n - 1) * group, d_vit), BF16),
            pltpu.SemaphoreType.DMA((len(operands),)),
        ],
        mib=62,
    )(*operands)
    outgoing = call(
        merge_kernel,
        jax.ShapeDtypeStruct((slots, width), BF16),
        [vmem] * 5 + [hbm, vmem, hbm],
        2 * patch_count * d_vit * width,
        scratch=[
            pltpu.VMEM((group, patch_count), BF16),
            pltpu.VMEM((group, d_vit), BF16),
            pltpu.VMEM((d_vit // 128, patch_count, 128), F32),
            pltpu.VMEM(merger_weight.shape[::-1], BF16),
            pltpu.VMEM((slots, width), BF16),
            pltpu.SemaphoreType.DMA((2,)),
        ],
        mib=62,
    )(
        contexts[n - 1],
        tall[-1],
        last,
        sofar,
        merge_gain[None, :],
        merger_weight.T,
        slot_column,
        from_audio,
    )
    down_turned, outgoing = lax.optimization_barrier((down_weight.T, outgoing))
    down_whole = lax.all_gather(down_turned, "dp", axis=0, tiled=True)
    incoming = lax.all_to_all(
        outgoing.reshape(owner_count, capacity, width), "dp", split_axis=0, concat_axis=0, tiled=True
    ).reshape(slots, width)
    taken_lengths = span_lengths[:, owner]
    arrival = span_time[owner]
    earlier = arrival[:, None] < arrival[None, :]
    offsets = jnp.sum(jnp.where(earlier, taken_lengths[:, None], 0), axis=0)
    target = jnp.where(
        slot_index[None, :] < taken_lengths[:, None], offsets[:, None] + slot_index[None, :], -1
    ).reshape(1, -1)
    sequence = call(
        pick_kernel,
        jax.ShapeDtypeStruct((seq_count, width), BF16),
        [vmem] * 2,
        2 * slots * seq_count * width,
        mib=16,
    )(target, incoming)

    features = n * width
    own_count = seq_count // n
    shifts = [0]
    for k in range(1, n // 2):
        shifts += [-k, k]
    shifts.append(-(n // 2))
    early = 5
    here = plane.reshape(1)
    padded = 2 * units + gap
    gains = llm_gain.reshape(n, 1, width)

    def scratch(count, sems):
        return [
            pltpu.VMEM((seq_count, count * width), BF16),
            pltpu.VMEM((count * width, padded), BF16),
            pltpu.VMEM((seq_count, padded), F32),
            pltpu.SemaphoreType.DMA((count + sems,)),
        ]

    blocks = [sequence]
    a = b = sequence
    for k in range(1, n // 2 + 1):
        a = lax.ppermute(a, "tensor", shifted("tensor", 1))
        if k < n // 2:
            b = lax.ppermute(b, "tensor", shifted("tensor", -1))
        if k == n // 2 - 1:
            sums, squares = call(
                functools.partial(early_kernel, shifts[:early]),
                (
                    jax.ShapeDtypeStruct((seq_count, padded), F32),
                    jax.ShapeDtypeStruct((seq_count, 1), F32),
                ),
                [smem] + [vmem] * (early + 1) + [hbm],
                4 * seq_count * early * width * units,
                scratch=scratch(early, padded // 256 + 1),
                mib=57,
                out_space=(HBM, VMEM),
            )(here, *blocks, gains, whole)
            a, b, sums = lax.optimization_barrier((a, b, sums))
        blocks.append(a)
        if k < n // 2:
            blocks.append(b)
    hidden, own_rows = call(
        functools.partial(late_kernel, shifts, early, units),
        (
            jax.ShapeDtypeStruct((seq_count, units), BF16),
            jax.ShapeDtypeStruct((n, own_count, width), BF16),
        ),
        [smem] + [vmem] * (n + 1) + [hbm] * 2 + [vmem],
        4 * seq_count * (n - early) * width * units,
        scratch=scratch(n - early, 1),
        mib=57,
    )(here, *blocks, gains, whole, sums, squares)
    tile = 512
    half = jax.ShapeDtypeStruct((seq_count // 2, features), BF16)
    scattered, ringed = call(
        functools.partial(down_kernel, tile, n),
        (half, half),
        [vmem, hbm],
        2 * seq_count * features * units,
        scratch=[
            pltpu.VMEM((features, units), BF16),
            pltpu.VMEM(half.shape, BF16),
            pltpu.VMEM(half.shape, BF16),
            pltpu.SemaphoreType.DMA((3 * (features // tile),)),
        ],
        mib=57,
        out_space=HBM,
    )(hidden, down_whole)
    by_scatter = lax.psum_scatter(scattered, "tensor", scatter_dimension=0, tiled=True).astype(F32)

    ringed = ringed.reshape(n, own_count // 2, features)

    def term(shift):
        return lax.dynamic_index_in_dim(ringed, lax.rem(plane + shift + n, n), 0, keepdims=False)

    def running(step, count):
        total = term(step * count)
        for k in range(count - 1, -1, -1):
            total = lax.ppermute(total, "tensor", shifted("tensor", step))
            if k > 0:
                total = (total.astype(F32) + term(step * k).astype(F32)).astype(BF16)
        return total.astype(F32)

    by_ring = term(0).astype(F32) + running(1, n // 2) + running(-1, n - n // 2 - 1)
    own_rows = jnp.moveaxis(own_rows, 0, 1).reshape(own_count, features).astype(F32)
    return (own_rows + jnp.concatenate([by_scatter, by_ring], axis=0)).astype(BF16)


def solution(mesh):
    return jax.shard_map(
        body,
        mesh=mesh,
        in_specs=(
            P("dp", None),
            P("dp", None),
            P(),
            P(None, None, "tensor"),
            P("tensor", None),
            P(),
            P(None, "tensor"),
            P("dp", "tensor"),
            P(),
            P(),
            P(),
            P("dp", "tensor"),
            P("dp", "tensor"),
            P("tensor", "dp"),
        ),
        out_specs=P(("dp", "tensor"), None),
        check_vma=False,
    )
```

```python
import functools
import math

import jax
import jax.numpy as jnp
from jax import lax
from jax.experimental import pallas as pl
from jax.experimental.pallas import tpu as pltpu
from jax.sharding import PartitionSpec as P

HEAD_VIT = 80
EPSILON = 1e-06
VMEM = pltpu.MemorySpace.VMEM
SMEM = pltpu.MemorySpace.SMEM
HBM = pltpu.MemorySpace.HBM
BF16 = jnp.bfloat16
F32 = jnp.float32


def shifted(axis, step):
    n = lax.axis_size(axis)
    return [(i, (i + step) % n) for i in range(n)]


def ring_blocks(x, axis):
    n = lax.axis_size(axis)
    blocks = {0: x}
    a = b = x
    for k in range(1, n // 2 + 1):
        a = lax.ppermute(a, axis, shifted(axis, 1))
        blocks[-k] = a
        if k < n - n // 2:
            b = lax.ppermute(b, axis, shifted(axis, -1))
            blocks[k] = b
    return blocks


def turned_dot(left, right):
    return lax.dot_general(left, right, (((1,), (1,)), ((), ())), preferred_element_type=F32)


def inverse_rms(wide):
    return lax.rsqrt(jnp.mean(wide * wide, axis=-1, keepdims=True) + EPSILON)


def vision_kernel(core_ref, patches_ref, column_ref, row_ref, gain_ref, weight_ref, out_ref):
    wide = patches_ref[...].astype(F32)
    normed = (wide * inverse_rms(wide) * gain_ref[...]).astype(BF16)
    query, keys, values = (
        turned_dot(normed, weight_ref[k]).astype(BF16) for k in range(3)
    )
    same = column_ref[...] == row_ref[...]
    for head in range(2):
        part = slice(head * HEAD_VIT, (head + 1) * HEAD_VIT)
        scores = turned_dot(query[:, part], keys[:, part])
        scores = jnp.where(same, scores * (1.0 / math.sqrt(HEAD_VIT)), -1e30)
        weights = jnp.exp(scores - jnp.max(scores, axis=-1, keepdims=True))
        probs = (weights / jnp.sum(weights, axis=-1, keepdims=True)).astype(BF16)
        context = lax.dot_general(
            values[:, part], probs, (((0,), (1,)), ((), ())), preferred_element_type=F32
        )
        place = pl.multiple_of(lax.rem(core_ref[0] + head, 2) * HEAD_VIT, 16)
        out_ref[pl.ds(place, HEAD_VIT), :] = context.astype(BF16)


def lay(into, at, wide):
    rows, columns = wide.shape
    for j in range(columns // 128):
        into[pl.ds(at + j * rows, rows), :] = wide[:, pl.ds(j * 128, 128)]


def spread(into, at, tall, start, rows):
    for j in range(into.shape[1] // 128):
        into[pl.ds(at, rows), pl.ds(j * 128, 128)] = tall[pl.ds(start + j * rows, rows), :]


def pack_kernel(context_ref, above_ref, below_ref, up_ref, down_ref):
    split = context_ref.size // 128
    for out_ref, block_ref in ((up_ref, above_ref), (down_ref, below_ref)):
        lay(out_ref, 0, context_ref)
        lay(out_ref, split, block_ref)


def stack_kernel(wide_count, *refs):
    blocks, out_ref = refs[:-1], refs[-1]
    rows = out_ref.shape[1]
    for k, ref in enumerate(blocks):
        if k < wide_count:
            lay(out_ref.at[k], 0, ref)
        else:
            out_ref[k] = ref[pl.ds(ref.shape[0] - rows, rows), :]


def project_kernel(n, *refs):
    count = n + 4
    sources, out_ref, sems = refs[:count], refs[count], refs[-1]
    places, (context, weight) = refs[count + 1 : 2 * count + 1], refs[2 * count + 1 : 2 * count + 3]
    fetch = [
        pltpu.make_async_copy(source, place, sems.at[k])
        for k, (source, place) in enumerate(zip(sources, places))
    ]
    for copy in fetch:
        copy.start()
    payloads, wide, (other, patches) = places[: n - 1], places[n - 1 : n + 2], places[n + 2 :]
    group = 2 * HEAD_VIT
    split = group * context.shape[1] // 128
    for k in range(n - 1):
        fetch[k].wait()
        spread(context, k * group, payloads[k], 0, group)
    for k in range(3):
        fetch[n - 1 + k].wait()
        weight[pl.ds(k * group, HEAD_VIT), :] = wide[k][...]
    for k in range(3, n - 1):
        spread(weight, k * group, payloads[k - 2], split, HEAD_VIT)
    turned = context[...].T
    fetch[n + 2].wait()
    for k in range(n - 1):
        spread(weight, k * group + HEAD_VIT, other.at[k], 0, HEAD_VIT)
    fetch[n + 3].wait()

    @pl.loop(0, out_ref.shape[1] // 256)
    def _(j):
        columns = pl.ds(pl.multiple_of(j * 256, 256), 256)
        attended = jnp.dot(turned, weight[:, columns], preferred_element_type=F32)
        out_ref[:, columns] = patches[:, columns].astype(F32) + attended


def merge_kernel(*refs):
    context_ref, mine_ref, last_ref, sofar_ref, gain_ref, merger_hbm, slot_ref, audio_hbm, out_ref = refs[:9]
    context, weight, normed, merger, audio, sems = refs[9:]
    fetch = [
        pltpu.make_async_copy(merger_hbm, merger, sems.at[0]),
        pltpu.make_async_copy(audio_hbm, audio, sems.at[1]),
    ]
    for copy in fetch:
        copy.start()
    rows, d_vit = sofar_ref.shape
    group = 2 * HEAD_VIT
    split = group * rows // 128
    spread(context, 0, context_ref, 0, group)
    spread(weight, 0, mine_ref, split, HEAD_VIT)
    spread(weight, HEAD_VIT, last_ref, split, HEAD_VIT)
    turned = context[...].T
    lanes = 128
    squares = jnp.zeros((rows, 1), F32)
    for j in range(d_vit // 256):
        columns = pl.ds(j * 256, 256)
        attended = jnp.dot(turned, weight[:, columns], preferred_element_type=F32)
        wide = (sofar_ref[:, columns] + attended).astype(BF16).astype(F32)
        squares += jnp.sum(wide * wide, axis=-1, keepdims=True)
        normed[2 * j] = wide[:, :lanes]
        normed[2 * j + 1] = wide[:, lanes:]
    scale = lax.rsqrt(squares / d_vit + EPSILON)
    for j in range(d_vit // lanes):
        normed[j] = normed[j] * scale * gain_ref[:, pl.ds(j * lanes, lanes)]

    fetch[0].wait()
    video = jnp.zeros((rows // 4, merger.shape[0]), F32)
    for j in range(4):
        part = [normed[k, pl.ds(j, rows // 4, stride=4), :] for k in range(d_vit // lanes)]
        part = jnp.concatenate(part, axis=1).astype(BF16)
        video += turned_dot(part, merger[:, pl.ds(j * d_vit, d_vit)])
    video = video.astype(BF16)
    index = lax.broadcasted_iota(jnp.int32, (slot_ref.shape[0], rows // 4), 1)
    select = (slot_ref[...] == index).astype(F32).astype(BF16)
    placed = jnp.dot(select, video, preferred_element_type=F32)
    fetch[1].wait()
    out_ref[...] = (placed + audio[...].astype(F32)).astype(BF16)


def pick_kernel(target_ref, incoming_ref, out_ref):
    row = lax.broadcasted_iota(jnp.int32, (out_ref.shape[0], incoming_ref.shape[0]), 0)
    pick = (row == target_ref[...]).astype(F32).astype(BF16)
    out_ref[...] = jnp.dot(pick, incoming_ref[...], preferred_element_type=F32).astype(BF16)


def tile_fetch(places, whole_hbm, whole, sems, tile):
    chunk = whole.shape[0] // len(places)
    tiles = pl.cdiv(whole.shape[1], tile)

    def fetch(j, start, size):
        columns = pl.ds(start, size)
        copies = []
        for k, at in enumerate(places):
            source = whole_hbm.at[pl.ds(pl.multiple_of(at * chunk, 16), chunk), columns]
            place = whole.at[pl.ds(k * chunk, chunk), columns]
            copies.append(pltpu.make_async_copy(source, place, sems.at[k * tiles + j]))
        return copies

    return fetch


def run(copies, what):
    for copy in copies:
        getattr(copy, what)()


def scaled_blocks(blocks, gains, scaled, squares):
    chunk = blocks[0].shape[1]
    for j, block in enumerate(blocks):
        wide = block[...].astype(F32)
        squares += jnp.sum(wide * wide, axis=-1, keepdims=True)
        scaled[:, pl.ds(j * chunk, chunk)] = (wide * gains[j]).astype(BF16)
    return squares


def early_kernel(shifts, place_ref, *refs):
    count = len(shifts)
    blocks, gain_ref, whole_hbm, sums_hbm, squares_ref = refs[:count], *refs[count : count + 4]
    scaled, whole, sums, sems = refs[count + 4 :]
    n, tile, width = gain_ref.shape[0], 256, sums.shape[1]
    places = [lax.rem(place_ref[0] + shift + n, n) for shift in shifts]
    fetch = tile_fetch(places, whole_hbm, whole, sems, tile)
    full, rest = width // tile, width % tile
    last = (full, full * tile, rest)

    def part(j):
        return j, pl.multiple_of(j * tile, tile), tile

    @pl.loop(0, full)
    def _(j):
        run(fetch(*part(j)), "start")

    run(fetch(*last), "start")
    zero = jnp.zeros((blocks[0].shape[0], 1), F32)
    squares_ref[...] = scaled_blocks(blocks, [gain_ref[at] for at in places], scaled, zero)

    def result(j, start, size):
        columns = pl.ds(start, size)
        place = sems.at[count * (full + 1) + j]
        return pltpu.make_async_copy(sums.at[:, columns], sums_hbm.at[:, columns], place)

    def step(j, start, size):
        run(fetch(j, start, size), "wait")
        columns = pl.ds(start, size)
        sums[:, columns] = jnp.dot(scaled[...], whole[:, columns], preferred_element_type=F32)
        result(j, start, size).start()

    @pl.loop(0, full)
    def _(j):
        step(*part(j))

    step(*last)

    @pl.loop(0, full)
    def _(j):
        result(*part(j)).wait()

    result(*last).wait()


def late_kernel(shifts, early, units, place_ref, *refs):
    n = len(shifts)
    blocks, gain_ref, whole_hbm, sums_hbm, squares_ref, hidden_ref, own_ref = refs[:n], *refs[n : n + 6]
    scaled, whole, sums, sems = refs[n + 6 :]
    tile = 256
    places = [lax.rem(place_ref[0] + shift + n, n) for shift in shifts]
    fetch = tile_fetch(places[early:], whole_hbm, whole, sems, tile)
    width = whole.shape[1]
    tiles = pl.cdiv(width, tile)
    apart = width - units
    full, rest = units // tile, units % tile

    def both(j, start, size):
        copies = []
        whole_tiles = size if size == tile else apart - full * tile
        for k, first, size in ((0, 0, whole_tiles), (full + 1, apart, size)):
            copies += fetch(k + j, first + start, size)
            columns = pl.ds(first + start, size)
            place = sems.at[(n - early) * tiles + k + j]
            copies.append(pltpu.make_async_copy(sums_hbm.at[:, columns], sums.at[:, columns], place))
        return copies

    last = (full, full * tile, rest)

    def part(j):
        return j, pl.multiple_of(j * tile, tile), tile

    @pl.loop(0, full)
    def _(j):
        run(both(*part(j)), "start")

    run(both(*last), "start")
    gains = [gain_ref[at] for at in places[early:]]
    squares = scaled_blocks(blocks[early:], gains, scaled, squares_ref[...])
    scale = lax.rsqrt(squares / whole_hbm.shape[0] + EPSILON)
    own = own_ref.shape[1]
    first = pl.multiple_of(place_ref[0] * own, own)
    for at, block in zip(places, blocks):
        own_ref[at] = block[pl.ds(first, own), :]

    def step(j, start, size):
        run(both(j, start, size), "wait")
        gate, upward = (
            scale
            * (
                sums[:, pl.ds(at, size)]
                + jnp.dot(scaled[...], whole[:, pl.ds(at, size)], preferred_element_type=F32)
            )
            for at in (start, apart + start)
        )
        value = gate * (1.0 / (1.0 + jnp.exp(-gate))) * upward
        hidden_ref[:, pl.ds(start, size)] = value.astype(BF16)

    @pl.loop(0, full)
    def _(j):
        step(*part(j))

    step(*last)


def down_kernel(tile, hidden_ref, weight_hbm, out_hbm, weight, out, sems):
    tiles = weight.shape[0] // tile

    def here(j):
        return pl.ds(pl.multiple_of(j * tile, tile), tile)

    def part(j):
        return pltpu.make_async_copy(weight_hbm.at[here(j), :], weight.at[here(j), :], sems.at[j])

    def result(j):
        return pltpu.make_async_copy(out.at[:, here(j)], out_hbm.at[:, here(j)], sems.at[tiles + j])

    @pl.loop(0, tiles)
    def _(j):
        part(j).start()

    @pl.loop(0, tiles)
    def _(j):
        part(j).wait()
        out[:, here(j)] = turned_dot(hidden_ref[...], weight[here(j), :]).astype(BF16)
        result(j).start()

    @pl.loop(0, tiles)
    def _(j):
        result(j).wait()


def call(kernel, out_shape, specs, flops, scratch=(), mib=16, out_space=VMEM):
    def run(*args):
        moved = sum(a.size * a.dtype.itemsize for a in args)
        if isinstance(out_shape, tuple):
            spaces = out_space if isinstance(out_space, tuple) else (out_space,) * len(out_shape)
            outs = tuple(pl.BlockSpec(memory_space=space) for space in spaces)
        else:
            outs = pl.BlockSpec(memory_space=out_space)
        return pl.pallas_call(
            kernel,
            out_shape=out_shape,
            in_specs=specs,
            out_specs=outs,
            scratch_shapes=scratch,
            compiler_params=pltpu.CompilerParams(vmem_limit_bytes=mib << 20),
            cost_estimate=pl.CostEstimate(flops=flops, bytes_accessed=moved, transcendentals=0),
        )(*args)

    return run


def body(
    patches,
    window_ids,
    vit_gain,
    qkv_weight,
    out_weight,
    merge_gain,
    merger_weight,
    audio,
    span_lengths,
    span_time,
    llm_gain,
    gate_weight,
    up_weight,
    down_weight,
):
    patch_count, d_vit = patches.shape
    n = lax.axis_size("tensor")
    owner_count = lax.axis_size("dp")
    owner = lax.axis_index("dp")
    plane = lax.axis_index("tensor")
    core = lax.rem(owner, 2)
    units = gate_weight.shape[1]
    vmem = pl.BlockSpec(memory_space=VMEM)
    smem = pl.BlockSpec(memory_space=SMEM)
    hbm = pl.BlockSpec(memory_space=HBM)

    windows = window_ids[0]
    context = call(
        vision_kernel,
        jax.ShapeDtypeStruct((2 * HEAD_VIT, patch_count), BF16),
        [smem] + [vmem] * 5,
        2 * patch_count * (3 * d_vit * 160 + 4 * patch_count * HEAD_VIT),
    )(
        core.reshape(1),
        patches,
        windows[:, None],
        windows[None, :],
        vit_gain[None, :],
        jnp.swapaxes(qkv_weight, 1, 2),
    )

    group = 2 * HEAD_VIT
    own_head = lax.dynamic_slice_in_dim(out_weight, core * HEAD_VIT, HEAD_VIT, 0)
    above = lax.ppermute(own_head, "tensor", shifted("tensor", 1))
    below = lax.ppermute(own_head, "tensor", shifted("tensor", -1))
    split, block_rows = group * patch_count // 128, HEAD_VIT * d_vit // 128
    payload = jax.ShapeDtypeStruct((split + block_rows, 128), BF16)
    up, down = call(pack_kernel, (payload, payload), [vmem] * 3, 0)(context, above, below)
    ups, downs = [up], [down]
    for k in range(1, n // 2):
        ups.append(lax.ppermute(ups[-1], "tensor", shifted("tensor", 1)))
        away = downs[-1] if k < n // 2 - 1 else downs[-1][:split]
        downs.append(lax.ppermute(away, "tensor", shifted("tensor", -1)))
    ups.append(lax.ppermute(ups[-1][:split], "tensor", shifted("tensor", 1)))
    contexts = [up]
    tall = []
    for k in range(1, n // 2 + 1):
        contexts.append(ups[k])
        if k < n // 2:
            contexts.append(downs[k])
            tall.append(ups[k])
        if k < n // 2 - 1:
            tall.append(downs[k])
    swap = [(i, i ^ 1) for i in range(owner_count)]
    laid = call(
        functools.partial(stack_kernel, 3),
        jax.ShapeDtypeStruct((n - 1, block_rows, 128), BF16),
        [vmem] * (n - 1),
        0,
    )(own_head, above, below, *tall[:-1])
    other = lax.ppermute(laid, "dp", swap)
    last = lax.ppermute(tall[-1], "dp", swap)

    gap = -units % 128
    stacked = jnp.concatenate(
        [gate_weight, jnp.zeros((gate_weight.shape[0], gap), BF16), up_weight], axis=1
    )
    whole = lax.all_gather(stacked, "dp", axis=0, tiled=True)

    video_rows = patch_count // 4
    seq_count = video_rows + audio.shape[0]
    capacity = 2 * seq_count // owner_count
    sent_lengths = span_lengths[owner]
    starts = jnp.cumsum(sent_lengths) - sent_lengths
    slot_index = jnp.arange(capacity, dtype=jnp.int32)
    row_of_slot = jnp.where(
        slot_index[None, :] < sent_lengths[:, None], starts[:, None] + slot_index[None, :], -1
    ).reshape(-1)
    row = jnp.arange(seq_count, dtype=jnp.int32)
    select = (row_of_slot[:, None] == row[None, video_rows:]).astype(BF16)
    from_audio = jnp.dot(select, audio, preferred_element_type=F32).astype(BF16)
    slots = owner_count * capacity
    width = audio.shape[1]
    operands = [*contexts[: n - 1], own_head, above, below, other, patches]
    sofar = call(
        functools.partial(project_kernel, n),
        jax.ShapeDtypeStruct((patch_count, d_vit), F32),
        [hbm] * len(operands),
        2 * patch_count * d_vit * d_vit,
        scratch=[pltpu.VMEM(a.shape, BF16) for a in operands]
        + [
            pltpu.VMEM(((n - 1) * group, patch_count), BF16),
            pltpu.VMEM(((n - 1) * group, d_vit), BF16),
            pltpu.SemaphoreType.DMA((len(operands),)),
        ],
        mib=62,
    )(*operands)
    outgoing = call(
        merge_kernel,
        jax.ShapeDtypeStruct((slots, width), BF16),
        [vmem] * 5 + [hbm, vmem, hbm],
        2 * patch_count * d_vit * width,
        scratch=[
            pltpu.VMEM((group, patch_count), BF16),
            pltpu.VMEM((group, d_vit), BF16),
            pltpu.VMEM((d_vit // 128, patch_count, 128), F32),
            pltpu.VMEM(merger_weight.shape[::-1], BF16),
            pltpu.VMEM((slots, width), BF16),
            pltpu.SemaphoreType.DMA((2,)),
        ],
        mib=62,
    )(
        contexts[n - 1],
        tall[-1],
        last,
        sofar,
        merge_gain[None, :],
        merger_weight.T,
        row_of_slot[:, None],
        from_audio,
    )
    down_turned, outgoing = lax.optimization_barrier((down_weight.T, outgoing))
    down_whole = lax.all_gather(down_turned, "dp", axis=0, tiled=True)
    incoming = lax.all_to_all(
        outgoing.reshape(owner_count, capacity, width), "dp", split_axis=0, concat_axis=0, tiled=True
    ).reshape(slots, width)
    taken_lengths = span_lengths[:, owner]
    arrival = span_time[owner]
    earlier = arrival[:, None] < arrival[None, :]
    offsets = jnp.sum(jnp.where(earlier, taken_lengths[:, None], 0), axis=0)
    target = jnp.where(
        slot_index[None, :] < taken_lengths[:, None], offsets[:, None] + slot_index[None, :], -1
    ).reshape(1, -1)
    sequence = call(
        pick_kernel,
        jax.ShapeDtypeStruct((seq_count, width), BF16),
        [vmem] * 2,
        2 * slots * seq_count * width,
        mib=16,
    )(target, incoming)

    features = n * width
    own_count = seq_count // n
    shifts = [0]
    for k in range(1, n // 2):
        shifts += [-k, k]
    shifts.append(-(n // 2))
    early = 5
    here = plane.reshape(1)
    padded = 2 * units + gap
    gains = llm_gain.reshape(n, 1, width)
    tiles = pl.cdiv(padded, 256)

    def scratch(count):
        return [
            pltpu.VMEM((seq_count, count * width), BF16),
            pltpu.VMEM((count * width, padded), BF16),
            pltpu.VMEM((seq_count, padded), F32),
            pltpu.SemaphoreType.DMA(((count + 1) * tiles,)),
        ]

    blocks = [sequence]
    a = b = sequence
    for k in range(1, n // 2 + 1):
        a = lax.ppermute(a, "tensor", shifted("tensor", 1))
        if k < n // 2:
            b = lax.ppermute(b, "tensor", shifted("tensor", -1))
        if k == n // 2 - 1:
            sums, squares = call(
                functools.partial(early_kernel, shifts[:early]),
                (
                    jax.ShapeDtypeStruct((seq_count, padded), F32),
                    jax.ShapeDtypeStruct((seq_count, 1), F32),
                ),
                [smem] + [vmem] * (early + 1) + [hbm],
                4 * seq_count * early * width * units,
                scratch=scratch(early),
                mib=48,
                out_space=(HBM, VMEM),
            )(here, *blocks, gains, whole)
            a, b, sums = lax.optimization_barrier((a, b, sums))
        blocks.append(a)
        if k < n // 2:
            blocks.append(b)
    hidden, own_rows = call(
        functools.partial(late_kernel, shifts, early, units),
        (
            jax.ShapeDtypeStruct((seq_count, units), BF16),
            jax.ShapeDtypeStruct((n, own_count, width), BF16),
        ),
        [smem] + [vmem] * (n + 1) + [hbm] * 2 + [vmem],
        4 * seq_count * (n - early) * width * units,
        scratch=scratch(n - early),
        mib=48,
    )(here, *blocks, gains, whole, sums, squares)
    down_tile = 512
    terms = call(
        functools.partial(down_kernel, down_tile),
        jax.ShapeDtypeStruct((seq_count, features), BF16),
        [vmem, hbm],
        2 * seq_count * features * units,
        scratch=[
            pltpu.VMEM((features, units), BF16),
            pltpu.VMEM((seq_count, features), BF16),
            pltpu.SemaphoreType.DMA((2 * (features // down_tile),)),
        ],
        mib=62,
        out_space=HBM,
    )(hidden, down_whole)
    summed = lax.psum_scatter(terms, "tensor", scatter_dimension=0, tiled=True).astype(F32)
    own_rows = jnp.moveaxis(own_rows, 0, 1).reshape(own_count, features)
    return (own_rows.astype(F32) + summed).astype(BF16)


def solution(mesh):
    return jax.shard_map(
        body,
        mesh=mesh,
        in_specs=(
            P("dp", None),
            P("dp", None),
            P(),
            P(None, None, "tensor"),
            P("tensor", None),
            P(),
            P(None, "tensor"),
            P("dp", "tensor"),
            P(),
            P(),
            P(),
            P("dp", "tensor"),
            P("dp", "tensor"),
            P("tensor", "dp"),
        ),
        out_specs=P(("dp", "tensor"), None),
        check_vma=False,
    )
```

```python
import functools
import math

import jax
import jax.numpy as jnp
from jax import lax
from jax.experimental import pallas as pl
from jax.experimental.pallas import tpu as pltpu
from jax.sharding import PartitionSpec as P

HEAD_VIT = 80
EPSILON = 1e-06
VMEM = pltpu.MemorySpace.VMEM
SMEM = pltpu.MemorySpace.SMEM
HBM = pltpu.MemorySpace.HBM
BF16 = jnp.bfloat16
F32 = jnp.float32


def shifted(axis, step):
    n = lax.axis_size(axis)
    return [(i, (i + step) % n) for i in range(n)]


def ring_blocks(x, axis):
    n = lax.axis_size(axis)
    blocks = {0: x}
    a = b = x
    for k in range(1, n // 2 + 1):
        a = lax.ppermute(a, axis, shifted(axis, 1))
        blocks[-k] = a
        if k < n - n // 2:
            b = lax.ppermute(b, axis, shifted(axis, -1))
            blocks[k] = b
    return blocks


def turned_dot(left, right):
    return lax.dot_general(left, right, (((1,), (1,)), ((), ())), preferred_element_type=F32)


def inverse_rms(wide):
    return lax.rsqrt(jnp.mean(wide * wide, axis=-1, keepdims=True) + EPSILON)


def vision_kernel(core_ref, patches_ref, column_ref, row_ref, gain_ref, weight_ref, out_ref):
    wide = patches_ref[...].astype(F32)
    normed = (wide * inverse_rms(wide) * gain_ref[...]).astype(BF16)
    query, keys, values = (
        turned_dot(normed, weight_ref[k]).astype(BF16) for k in range(3)
    )
    same = column_ref[...] == row_ref[...]
    for head in range(2):
        part = slice(head * HEAD_VIT, (head + 1) * HEAD_VIT)
        scores = turned_dot(query[:, part], keys[:, part])
        scores = jnp.where(same, scores * (1.0 / math.sqrt(HEAD_VIT)), -1e30)
        weights = jnp.exp(scores - jnp.max(scores, axis=-1, keepdims=True))
        probs = (weights / jnp.sum(weights, axis=-1, keepdims=True)).astype(BF16)
        context = lax.dot_general(
            values[:, part], probs, (((0,), (1,)), ((), ())), preferred_element_type=F32
        )
        place = pl.multiple_of(lax.rem(core_ref[0] + head, 2) * HEAD_VIT, 16)
        out_ref[pl.ds(place, HEAD_VIT), :] = context.astype(BF16)


def lay(into, at, wide):
    rows, columns = wide.shape
    for j in range(columns // 128):
        into[pl.ds(at + j * rows, rows), :] = wide[:, pl.ds(j * 128, 128)]


def spread(into, at, tall, start, rows):
    for j in range(into.shape[1] // 128):
        into[pl.ds(at, rows), pl.ds(j * 128, 128)] = tall[pl.ds(start + j * rows, rows), :]


def pack_kernel(context_ref, above_ref, below_ref, up_ref, down_ref):
    split = context_ref.size // 128
    for out_ref, block_ref in ((up_ref, above_ref), (down_ref, below_ref)):
        lay(out_ref, 0, context_ref)
        lay(out_ref, split, block_ref)


def stack_kernel(wide_count, *refs):
    blocks, out_ref = refs[:-1], refs[-1]
    rows = out_ref.shape[1]
    for k, ref in enumerate(blocks):
        if k < wide_count:
            lay(out_ref.at[k], 0, ref)
        else:
            out_ref[k] = ref[pl.ds(ref.shape[0] - rows, rows), :]


def project_kernel(n, *refs):
    count = n + 4
    sources, out_ref, sems = refs[:count], refs[count], refs[-1]
    places, (context, weight) = refs[count + 1 : 2 * count + 1], refs[2 * count + 1 : 2 * count + 3]
    fetch = [
        pltpu.make_async_copy(source, place, sems.at[k])
        for k, (source, place) in enumerate(zip(sources, places))
    ]
    for copy in fetch:
        copy.start()
    payloads, wide, (other, patches) = places[: n - 1], places[n - 1 : n + 2], places[n + 2 :]
    group = 2 * HEAD_VIT
    split = group * context.shape[1] // 128
    for k in range(n - 1):
        fetch[k].wait()
        spread(context, k * group, payloads[k], 0, group)
    for k in range(3):
        fetch[n - 1 + k].wait()
        weight[pl.ds(k * group, HEAD_VIT), :] = wide[k][...]
    for k in range(3, n - 1):
        spread(weight, k * group, payloads[k - 2], split, HEAD_VIT)
    turned = context[...].T
    fetch[n + 2].wait()
    for k in range(n - 1):
        spread(weight, k * group + HEAD_VIT, other.at[k], 0, HEAD_VIT)
    fetch[n + 3].wait()

    @pl.loop(0, out_ref.shape[1] // 256)
    def _(j):
        columns = pl.ds(pl.multiple_of(j * 256, 256), 256)
        attended = jnp.dot(turned, weight[:, columns], preferred_element_type=F32)
        out_ref[:, columns] = patches[:, columns].astype(F32) + attended


def merge_kernel(*refs):
    context_ref, mine_ref, last_ref, sofar_ref, gain_ref, merger_hbm, slot_ref, audio_hbm, out_ref = refs[:9]
    context, weight, normed, merger, audio, sems = refs[9:]
    fetch = [
        pltpu.make_async_copy(merger_hbm, merger, sems.at[0]),
        pltpu.make_async_copy(audio_hbm, audio, sems.at[1]),
    ]
    for copy in fetch:
        copy.start()
    rows, d_vit = sofar_ref.shape
    group = 2 * HEAD_VIT
    split = group * rows // 128
    spread(context, 0, context_ref, 0, group)
    spread(weight, 0, mine_ref, split, HEAD_VIT)
    spread(weight, HEAD_VIT, last_ref, split, HEAD_VIT)
    turned = context[...].T
    lanes = 128
    squares = jnp.zeros((rows, 1), F32)
    for j in range(d_vit // 256):
        columns = pl.ds(j * 256, 256)
        attended = jnp.dot(turned, weight[:, columns], preferred_element_type=F32)
        wide = (sofar_ref[:, columns] + attended).astype(BF16).astype(F32)
        squares += jnp.sum(wide * wide, axis=-1, keepdims=True)
        normed[2 * j] = wide[:, :lanes]
        normed[2 * j + 1] = wide[:, lanes:]
    scale = lax.rsqrt(squares / d_vit + EPSILON)
    for j in range(d_vit // lanes):
        normed[j] = normed[j] * scale * gain_ref[:, pl.ds(j * lanes, lanes)]

    fetch[0].wait()
    video = jnp.zeros((rows // 4, merger.shape[0]), F32)
    for j in range(4):
        part = [normed[k, pl.ds(j, rows // 4, stride=4), :] for k in range(d_vit // lanes)]
        part = jnp.concatenate(part, axis=1).astype(BF16)
        video += turned_dot(part, merger[:, pl.ds(j * d_vit, d_vit)])
    video = video.astype(BF16)
    index = lax.broadcasted_iota(jnp.int32, (slot_ref.shape[0], rows // 4), 1)
    select = (slot_ref[...] == index).astype(F32).astype(BF16)
    placed = jnp.dot(select, video, preferred_element_type=F32)
    fetch[1].wait()
    out_ref[...] = (placed + audio[...].astype(F32)).astype(BF16)


def pick_kernel(target_ref, incoming_ref, out_ref):
    row = lax.broadcasted_iota(jnp.int32, (out_ref.shape[0], incoming_ref.shape[0]), 0)
    pick = (row == target_ref[...]).astype(F32).astype(BF16)
    out_ref[...] = jnp.dot(pick, incoming_ref[...], preferred_element_type=F32).astype(BF16)


def tile_fetch(places, whole_hbm, whole, sems, tile):
    chunk = whole.shape[0] // len(places)
    tiles = pl.cdiv(whole.shape[1], tile)

    def fetch(j, start, size):
        columns = pl.ds(start, size)
        copies = []
        for k, at in enumerate(places):
            source = whole_hbm.at[pl.ds(pl.multiple_of(at * chunk, 16), chunk), columns]
            place = whole.at[pl.ds(k * chunk, chunk), columns]
            copies.append(pltpu.make_async_copy(source, place, sems.at[k * tiles + j]))
        return copies

    return fetch


def run(copies, what):
    for copy in copies:
        getattr(copy, what)()


def scaled_blocks(blocks, gains, scaled, squares):
    chunk = blocks[0].shape[1]
    for j, block in enumerate(blocks):
        wide = block[...].astype(F32)
        squares += jnp.sum(wide * wide, axis=-1, keepdims=True)
        scaled[:, pl.ds(j * chunk, chunk)] = (wide * gains[j]).astype(BF16)
    return squares


def early_kernel(shifts, follows, place_ref, *refs):
    count = len(shifts)
    blocks, gain_ref, whole_hbm = refs[:count], refs[count], refs[count + 1]
    before = refs[count + 2 : count + 4] if follows else None
    sums_hbm, squares_ref, scaled, whole, sums, sems = refs[count + 2 + 2 * follows :]
    n, tile, width = gain_ref.shape[0], 256, sums.shape[1]
    places = [lax.rem(place_ref[0] + shift + n, n) for shift in shifts]
    fetch = tile_fetch(places, whole_hbm, whole, sems, tile)
    full, rest = width // tile, width % tile
    last = (full, full * tile, rest)

    def part(j):
        return j, pl.multiple_of(j * tile, tile), tile

    def operands(j, start, size):
        copies = fetch(j, start, size)
        if follows:
            columns = pl.ds(start, size)
            place = sems.at[(count + 1) * (full + 1) + j]
            copies.append(pltpu.make_async_copy(before[0].at[:, columns], sums.at[:, columns], place))
        return copies

    @pl.loop(0, full)
    def _(j):
        run(operands(*part(j)), "start")

    run(operands(*last), "start")
    squares = before[1][...] if follows else jnp.zeros((blocks[0].shape[0], 1), F32)
    squares_ref[...] = scaled_blocks(blocks, [gain_ref[at] for at in places], scaled, squares)

    def result(j, start, size):
        columns = pl.ds(start, size)
        place = sems.at[count * (full + 1) + j]
        return pltpu.make_async_copy(sums.at[:, columns], sums_hbm.at[:, columns], place)

    def step(j, start, size):
        run(operands(j, start, size), "wait")
        columns = pl.ds(start, size)
        total = jnp.dot(scaled[...], whole[:, columns], preferred_element_type=F32)
        sums[:, columns] = sums[:, columns] + total if follows else total
        result(j, start, size).start()

    @pl.loop(0, full)
    def _(j):
        step(*part(j))

    step(*last)

    @pl.loop(0, full)
    def _(j):
        result(*part(j)).wait()

    result(*last).wait()


def late_kernel(shifts, early, units, place_ref, *refs):
    n = len(shifts)
    blocks, gain_ref, whole_hbm, sums_hbm, squares_ref, hidden_ref, own_ref = refs[:n], *refs[n : n + 6]
    scaled, whole, sums, sems = refs[n + 6 :]
    tile = 256
    places = [lax.rem(place_ref[0] + shift + n, n) for shift in shifts]
    fetch = tile_fetch(places[early:], whole_hbm, whole, sems, tile)
    width = whole.shape[1]
    tiles = pl.cdiv(width, tile)
    apart = width - units
    full, rest = units // tile, units % tile

    def both(j, start, size):
        copies = []
        whole_tiles = size if size == tile else apart - full * tile
        for k, first, size in ((0, 0, whole_tiles), (full + 1, apart, size)):
            copies += fetch(k + j, first + start, size)
            columns = pl.ds(first + start, size)
            place = sems.at[(n - early) * tiles + k + j]
            copies.append(pltpu.make_async_copy(sums_hbm.at[:, columns], sums.at[:, columns], place))
        return copies

    last = (full, full * tile, rest)

    def part(j):
        return j, pl.multiple_of(j * tile, tile), tile

    @pl.loop(0, full)
    def _(j):
        run(both(*part(j)), "start")

    run(both(*last), "start")
    gains = [gain_ref[at] for at in places[early:]]
    squares = scaled_blocks(blocks[early:], gains, scaled, squares_ref[...])
    scale = lax.rsqrt(squares / whole_hbm.shape[0] + EPSILON)
    own = own_ref.shape[1]
    first = pl.multiple_of(place_ref[0] * own, own)
    for at, block in zip(places, blocks):
        own_ref[at] = block[pl.ds(first, own), :]

    def step(j, start, size):
        run(both(j, start, size), "wait")
        gate, upward = (
            scale
            * (
                sums[:, pl.ds(at, size)]
                + jnp.dot(scaled[...], whole[:, pl.ds(at, size)], preferred_element_type=F32)
            )
            for at in (start, apart + start)
        )
        value = gate * (1.0 / (1.0 + jnp.exp(-gate))) * upward
        hidden_ref[:, pl.ds(start, size)] = value.astype(BF16)

    @pl.loop(0, full)
    def _(j):
        step(*part(j))

    step(*last)


def down_kernel(tile, hidden_ref, weight_hbm, out_hbm, weight, out, sems):
    tiles = weight.shape[0] // tile

    def here(j):
        return pl.ds(pl.multiple_of(j * tile, tile), tile)

    def part(j):
        return pltpu.make_async_copy(weight_hbm.at[here(j), :], weight.at[here(j), :], sems.at[j])

    def result(j):
        return pltpu.make_async_copy(out.at[:, here(j)], out_hbm.at[:, here(j)], sems.at[tiles + j])

    @pl.loop(0, tiles)
    def _(j):
        part(j).start()

    @pl.loop(0, tiles)
    def _(j):
        part(j).wait()
        out[:, here(j)] = turned_dot(hidden_ref[...], weight[here(j), :]).astype(BF16)
        result(j).start()

    @pl.loop(0, tiles)
    def _(j):
        result(j).wait()


def call(kernel, out_shape, specs, flops, scratch=(), mib=16, out_space=VMEM):
    def run(*args):
        moved = sum(a.size * a.dtype.itemsize for a in args)
        if isinstance(out_shape, tuple):
            spaces = out_space if isinstance(out_space, tuple) else (out_space,) * len(out_shape)
            outs = tuple(pl.BlockSpec(memory_space=space) for space in spaces)
        else:
            outs = pl.BlockSpec(memory_space=out_space)
        return pl.pallas_call(
            kernel,
            out_shape=out_shape,
            in_specs=specs,
            out_specs=outs,
            scratch_shapes=scratch,
            compiler_params=pltpu.CompilerParams(vmem_limit_bytes=mib << 20),
            cost_estimate=pl.CostEstimate(flops=flops, bytes_accessed=moved, transcendentals=0),
        )(*args)

    return run


def body(
    patches,
    window_ids,
    vit_gain,
    qkv_weight,
    out_weight,
    merge_gain,
    merger_weight,
    audio,
    span_lengths,
    span_time,
    llm_gain,
    gate_weight,
    up_weight,
    down_weight,
):
    patch_count, d_vit = patches.shape
    n = lax.axis_size("tensor")
    owner_count = lax.axis_size("dp")
    owner = lax.axis_index("dp")
    plane = lax.axis_index("tensor")
    core = lax.rem(owner, 2)
    units = gate_weight.shape[1]
    vmem = pl.BlockSpec(memory_space=VMEM)
    smem = pl.BlockSpec(memory_space=SMEM)
    hbm = pl.BlockSpec(memory_space=HBM)

    windows = window_ids[0]
    context = call(
        vision_kernel,
        jax.ShapeDtypeStruct((2 * HEAD_VIT, patch_count), BF16),
        [smem] + [vmem] * 5,
        2 * patch_count * (3 * d_vit * 160 + 4 * patch_count * HEAD_VIT),
    )(
        core.reshape(1),
        patches,
        windows[:, None],
        windows[None, :],
        vit_gain[None, :],
        jnp.swapaxes(qkv_weight, 1, 2),
    )

    group = 2 * HEAD_VIT
    own_head = lax.dynamic_slice_in_dim(out_weight, core * HEAD_VIT, HEAD_VIT, 0)
    above = lax.ppermute(own_head, "tensor", shifted("tensor", 1))
    below = lax.ppermute(own_head, "tensor", shifted("tensor", -1))
    split, block_rows = group * patch_count // 128, HEAD_VIT * d_vit // 128
    payload = jax.ShapeDtypeStruct((split + block_rows, 128), BF16)
    up, down = call(pack_kernel, (payload, payload), [vmem] * 3, 0)(context, above, below)
    ups, downs = [up], [down]
    for k in range(1, n // 2):
        ups.append(lax.ppermute(ups[-1], "tensor", shifted("tensor", 1)))
        away = downs[-1] if k < n // 2 - 1 else downs[-1][:split]
        downs.append(lax.ppermute(away, "tensor", shifted("tensor", -1)))
    ups.append(lax.ppermute(ups[-1][:split], "tensor", shifted("tensor", 1)))
    contexts = [up]
    tall = []
    for k in range(1, n // 2 + 1):
        contexts.append(ups[k])
        if k < n // 2:
            contexts.append(downs[k])
            tall.append(ups[k])
        if k < n // 2 - 1:
            tall.append(downs[k])
    swap = [(i, i ^ 1) for i in range(owner_count)]
    laid = call(
        functools.partial(stack_kernel, 3),
        jax.ShapeDtypeStruct((n - 1, block_rows, 128), BF16),
        [vmem] * (n - 1),
        0,
    )(own_head, above, below, *tall[:-1])
    other = lax.ppermute(laid, "dp", swap)
    last = lax.ppermute(tall[-1], "dp", swap)

    gap = -units % 128
    stacked = jnp.concatenate(
        [gate_weight, jnp.zeros((gate_weight.shape[0], gap), BF16), up_weight], axis=1
    )
    whole = lax.all_gather(stacked, "dp", axis=0, tiled=True)

    video_rows = patch_count // 4
    seq_count = video_rows + audio.shape[0]
    capacity = 2 * seq_count // owner_count
    sent_lengths = span_lengths[owner]
    starts = jnp.cumsum(sent_lengths) - sent_lengths
    slot_index = jnp.arange(capacity, dtype=jnp.int32)
    row_of_slot = jnp.where(
        slot_index[None, :] < sent_lengths[:, None], starts[:, None] + slot_index[None, :], -1
    ).reshape(-1)
    row = jnp.arange(seq_count, dtype=jnp.int32)
    select = (row_of_slot[:, None] == row[None, video_rows:]).astype(BF16)
    from_audio = jnp.dot(select, audio, preferred_element_type=F32).astype(BF16)
    slots = owner_count * capacity
    width = audio.shape[1]
    operands = [*contexts[: n - 1], own_head, above, below, other, patches]
    sofar = call(
        functools.partial(project_kernel, n),
        jax.ShapeDtypeStruct((patch_count, d_vit), F32),
        [hbm] * len(operands),
        2 * patch_count * d_vit * d_vit,
        scratch=[pltpu.VMEM(a.shape, BF16) for a in operands]
        + [
            pltpu.VMEM(((n - 1) * group, patch_count), BF16),
            pltpu.VMEM(((n - 1) * group, d_vit), BF16),
            pltpu.SemaphoreType.DMA((len(operands),)),
        ],
        mib=62,
    )(*operands)
    outgoing = call(
        merge_kernel,
        jax.ShapeDtypeStruct((slots, width), BF16),
        [vmem] * 5 + [hbm, vmem, hbm],
        2 * patch_count * d_vit * width,
        scratch=[
            pltpu.VMEM((group, patch_count), BF16),
            pltpu.VMEM((group, d_vit), BF16),
            pltpu.VMEM((d_vit // 128, patch_count, 128), F32),
            pltpu.VMEM(merger_weight.shape[::-1], BF16),
            pltpu.VMEM((slots, width), BF16),
            pltpu.SemaphoreType.DMA((2,)),
        ],
        mib=62,
    )(
        contexts[n - 1],
        tall[-1],
        last,
        sofar,
        merge_gain[None, :],
        merger_weight.T,
        row_of_slot[:, None],
        from_audio,
    )
    down_turned, outgoing = lax.optimization_barrier((down_weight.T, outgoing))
    down_whole = lax.all_gather(down_turned, "dp", axis=0, tiled=True)
    incoming = lax.all_to_all(
        outgoing.reshape(owner_count, capacity, width), "dp", split_axis=0, concat_axis=0, tiled=True
    ).reshape(slots, width)
    taken_lengths = span_lengths[:, owner]
    arrival = span_time[owner]
    earlier = arrival[:, None] < arrival[None, :]
    offsets = jnp.sum(jnp.where(earlier, taken_lengths[:, None], 0), axis=0)
    target = jnp.where(
        slot_index[None, :] < taken_lengths[:, None], offsets[:, None] + slot_index[None, :], -1
    ).reshape(1, -1)
    sequence = call(
        pick_kernel,
        jax.ShapeDtypeStruct((seq_count, width), BF16),
        [vmem] * 2,
        2 * slots * seq_count * width,
        mib=16,
    )(target, incoming)

    features = n * width
    own_count = seq_count // n
    shifts = [0]
    for k in range(1, n // 2):
        shifts += [-k, k]
    shifts.append(-(n // 2))
    stages = ((0, 5), (5, 7))
    early = stages[-1][1]
    here = plane.reshape(1)
    padded = 2 * units + gap
    gains = llm_gain.reshape(n, 1, width)
    tiles = pl.cdiv(padded, 256)

    def scratch(count):
        return [
            pltpu.VMEM((seq_count, count * width), BF16),
            pltpu.VMEM((count * width, padded), BF16),
            pltpu.VMEM((seq_count, padded), F32),
            pltpu.SemaphoreType.DMA(((count + 2) * tiles,)),
        ]

    def products(first, last, blocks, before):
        return call(
            functools.partial(early_kernel, shifts[first:last], len(before) // 2),
            (
                jax.ShapeDtypeStruct((seq_count, padded), F32),
                jax.ShapeDtypeStruct((seq_count, 1), F32),
            ),
            [smem] + [vmem] * (last - first + 1) + [hbm] + [hbm, vmem][: len(before)],
            4 * seq_count * (last - first) * width * units,
            scratch=scratch(last - first),
            mib=48,
            out_space=(HBM, VMEM),
        )(here, *blocks[first:last], gains, whole, *before)

    blocks = [sequence]
    sums = ()
    a = b = sequence
    for k in range(1, n // 2 + 1):
        a = lax.ppermute(a, "tensor", shifted("tensor", 1))
        if k < n // 2:
            b = lax.ppermute(b, "tensor", shifted("tensor", -1))
        if k >= n // 2 - 1:
            sums = products(*stages[k - n // 2 + 1], blocks, tuple(sums))
            a, b, sums = lax.optimization_barrier((a, b, sums))
        blocks.append(a)
        if k < n // 2:
            blocks.append(b)
    hidden, own_rows = call(
        functools.partial(late_kernel, shifts, early, units),
        (
            jax.ShapeDtypeStruct((seq_count, units), BF16),
            jax.ShapeDtypeStruct((n, own_count, width), BF16),
        ),
        [smem] + [vmem] * (n + 1) + [hbm] * 2 + [vmem],
        4 * seq_count * (n - early) * width * units,
        scratch=scratch(n - early),
        mib=48,
    )(here, *blocks, gains, whole, *sums)
    down_tile = 512
    terms = call(
        functools.partial(down_kernel, down_tile),
        jax.ShapeDtypeStruct((seq_count, features), BF16),
        [vmem, hbm],
        2 * seq_count * features * units,
        scratch=[
            pltpu.VMEM((features, units), BF16),
            pltpu.VMEM((seq_count, features), BF16),
            pltpu.SemaphoreType.DMA((2 * (features // down_tile),)),
        ],
        mib=62,
        out_space=HBM,
    )(hidden, down_whole)
    summed = lax.psum_scatter(terms, "tensor", scatter_dimension=0, tiled=True).astype(F32)
    own_rows = jnp.moveaxis(own_rows, 0, 1).reshape(own_count, features)
    return (own_rows.astype(F32) + summed).astype(BF16)


def solution(mesh):
    return jax.shard_map(
        body,
        mesh=mesh,
        in_specs=(
            P("dp", None),
            P("dp", None),
            P(),
            P(None, None, "tensor"),
            P("tensor", None),
            P(),
            P(None, "tensor"),
            P("dp", "tensor"),
            P(),
            P(),
            P(),
            P("dp", "tensor"),
            P("dp", "tensor"),
            P("tensor", "dp"),
        ),
        out_specs=P(("dp", "tensor"), None),
        check_vma=False,
    )
```

```python
import functools
import math

import jax
import jax.numpy as jnp
from jax import lax
from jax.experimental import pallas as pl
from jax.experimental.pallas import tpu as pltpu
from jax.sharding import PartitionSpec as P

HEAD_VIT = 80
EPSILON = 1e-06
VMEM = pltpu.MemorySpace.VMEM
SMEM = pltpu.MemorySpace.SMEM
HBM = pltpu.MemorySpace.HBM
BF16 = jnp.bfloat16
F32 = jnp.float32


def shifted(axis, step):
    n = lax.axis_size(axis)
    return [(i, (i + step) % n) for i in range(n)]


def ring_blocks(x, axis):
    n = lax.axis_size(axis)
    blocks = {0: x}
    a = b = x
    for k in range(1, n // 2 + 1):
        a = lax.ppermute(a, axis, shifted(axis, 1))
        blocks[-k] = a
        if k < n - n // 2:
            b = lax.ppermute(b, axis, shifted(axis, -1))
            blocks[k] = b
    return blocks


def turned_dot(left, right):
    return lax.dot_general(left, right, (((1,), (1,)), ((), ())), preferred_element_type=F32)


def inverse_rms(wide):
    return lax.rsqrt(jnp.mean(wide * wide, axis=-1, keepdims=True) + EPSILON)


def vision_kernel(core_ref, patches_ref, column_ref, row_ref, gain_ref, weight_ref, out_ref):
    wide = patches_ref[...].astype(F32)
    normed = (wide * inverse_rms(wide) * gain_ref[...]).astype(BF16)
    query, keys, values = (
        turned_dot(normed, weight_ref[k]).astype(BF16) for k in range(3)
    )
    same = column_ref[...] == row_ref[...]
    for head in range(2):
        part = slice(head * HEAD_VIT, (head + 1) * HEAD_VIT)
        scores = turned_dot(query[:, part], keys[:, part])
        scores = jnp.where(same, scores * (1.0 / math.sqrt(HEAD_VIT)), -1e30)
        weights = jnp.exp(scores - jnp.max(scores, axis=-1, keepdims=True))
        probs = (weights / jnp.sum(weights, axis=-1, keepdims=True)).astype(BF16)
        context = lax.dot_general(
            values[:, part], probs, (((0,), (1,)), ((), ())), preferred_element_type=F32
        )
        place = pl.multiple_of(lax.rem(core_ref[0] + head, 2) * HEAD_VIT, 16)
        out_ref[pl.ds(place, HEAD_VIT), :] = context.astype(BF16)


def lay(into, at, wide):
    rows, columns = wide.shape
    for j in range(columns // 128):
        into[pl.ds(at + j * rows, rows), :] = wide[:, pl.ds(j * 128, 128)]


def spread(into, at, tall, start, rows):
    for j in range(into.shape[1] // 128):
        into[pl.ds(at, rows), pl.ds(j * 128, 128)] = tall[pl.ds(start + j * rows, rows), :]


def pack_kernel(context_ref, above_ref, below_ref, up_ref, down_ref):
    split = context_ref.size // 128
    for out_ref, block_ref in ((up_ref, above_ref), (down_ref, below_ref)):
        lay(out_ref, 0, context_ref)
        lay(out_ref, split, block_ref)


def stack_kernel(wide_count, *refs):
    blocks, out_ref = refs[:-1], refs[-1]
    rows = out_ref.shape[1]
    for k, ref in enumerate(blocks):
        if k < wide_count:
            lay(out_ref.at[k], 0, ref)
        else:
            out_ref[k] = ref[pl.ds(ref.shape[0] - rows, rows), :]


def project_kernel(n, *refs):
    count = n + 4
    sources, out_ref, sems = refs[:count], refs[count], refs[-1]
    places, (context, weight) = refs[count + 1 : 2 * count + 1], refs[2 * count + 1 : 2 * count + 3]
    fetch = [
        pltpu.make_async_copy(source, place, sems.at[k])
        for k, (source, place) in enumerate(zip(sources, places))
    ]
    for copy in fetch:
        copy.start()
    payloads, wide, (other, patches) = places[: n - 1], places[n - 1 : n + 2], places[n + 2 :]
    group = 2 * HEAD_VIT
    split = group * context.shape[1] // 128
    for k in range(n - 1):
        fetch[k].wait()
        spread(context, k * group, payloads[k], 0, group)
    for k in range(3):
        fetch[n - 1 + k].wait()
        weight[pl.ds(k * group, HEAD_VIT), :] = wide[k][...]
    for k in range(3, n - 1):
        spread(weight, k * group, payloads[k - 2], split, HEAD_VIT)
    turned = context[...].T
    fetch[n + 2].wait()
    for k in range(n - 1):
        spread(weight, k * group + HEAD_VIT, other.at[k], 0, HEAD_VIT)
    fetch[n + 3].wait()

    @pl.loop(0, out_ref.shape[1] // 256)
    def _(j):
        columns = pl.ds(pl.multiple_of(j * 256, 256), 256)
        attended = jnp.dot(turned, weight[:, columns], preferred_element_type=F32)
        out_ref[:, columns] = patches[:, columns].astype(F32) + attended


def merge_kernel(*refs):
    context_ref, mine_ref, last_ref, sofar_ref, gain_ref, merger_hbm, slot_ref, audio_hbm, out_ref = refs[:9]
    context, weight, normed, merger, audio, sems = refs[9:]
    fetch = [
        pltpu.make_async_copy(merger_hbm, merger, sems.at[0]),
        pltpu.make_async_copy(audio_hbm, audio, sems.at[1]),
    ]
    for copy in fetch:
        copy.start()
    rows, d_vit = sofar_ref.shape
    group = 2 * HEAD_VIT
    split = group * rows // 128
    spread(context, 0, context_ref, 0, group)
    spread(weight, 0, mine_ref, split, HEAD_VIT)
    spread(weight, HEAD_VIT, last_ref, split, HEAD_VIT)
    turned = context[...].T
    lanes = 128
    squares = jnp.zeros((rows, 1), F32)
    for j in range(d_vit // 256):
        columns = pl.ds(j * 256, 256)
        attended = jnp.dot(turned, weight[:, columns], preferred_element_type=F32)
        wide = (sofar_ref[:, columns] + attended).astype(BF16).astype(F32)
        squares += jnp.sum(wide * wide, axis=-1, keepdims=True)
        normed[2 * j] = wide[:, :lanes]
        normed[2 * j + 1] = wide[:, lanes:]
    scale = lax.rsqrt(squares / d_vit + EPSILON)
    for j in range(d_vit // lanes):
        normed[j] = normed[j] * scale * gain_ref[:, pl.ds(j * lanes, lanes)]

    fetch[0].wait()
    video = jnp.zeros((rows // 4, merger.shape[0]), F32)
    for j in range(4):
        part = [normed[k, pl.ds(j, rows // 4, stride=4), :] for k in range(d_vit // lanes)]
        part = jnp.concatenate(part, axis=1).astype(BF16)
        video += turned_dot(part, merger[:, pl.ds(j * d_vit, d_vit)])
    video = video.astype(BF16)
    index = lax.broadcasted_iota(jnp.int32, (slot_ref.shape[0], rows // 4), 1)
    select = (slot_ref[...] == index).astype(F32).astype(BF16)
    placed = jnp.dot(select, video, preferred_element_type=F32)
    fetch[1].wait()
    out_ref[...] = (placed + audio[...].astype(F32)).astype(BF16)


def pick_kernel(target_ref, incoming_ref, out_ref):
    row = lax.broadcasted_iota(jnp.int32, (out_ref.shape[0], incoming_ref.shape[0]), 0)
    pick = (row == target_ref[...]).astype(F32).astype(BF16)
    out_ref[...] = jnp.dot(pick, incoming_ref[...], preferred_element_type=F32).astype(BF16)


def tile_fetch(places, whole_hbm, whole, sems, tile):
    chunk = whole.shape[0] // len(places)
    tiles = pl.cdiv(whole.shape[1], tile)

    def fetch(j, start, size):
        columns = pl.ds(start, size)
        copies = []
        for k, at in enumerate(places):
            source = whole_hbm.at[pl.ds(pl.multiple_of(at * chunk, 16), chunk), columns]
            place = whole.at[pl.ds(k * chunk, chunk), columns]
            copies.append(pltpu.make_async_copy(source, place, sems.at[k * tiles + j]))
        return copies

    return fetch


def run(copies, what):
    for copy in copies:
        getattr(copy, what)()


def scaled_blocks(blocks, gains, scaled, squares):
    chunk = blocks[0].shape[1]
    for j, block in enumerate(blocks):
        wide = block[...].astype(F32)
        squares += jnp.sum(wide * wide, axis=-1, keepdims=True)
        scaled[:, pl.ds(j * chunk, chunk)] = (wide * gains[j]).astype(BF16)
    return squares


def early_kernel(shifts, follows, place_ref, *refs):
    count = len(shifts)
    blocks, gain_ref, whole_hbm = refs[:count], refs[count], refs[count + 1]
    before = refs[count + 2 : count + 4] if follows else None
    sums_hbm, squares_ref, scaled, whole, sums, sems = refs[count + 2 + 2 * follows :]
    n, tile, width = gain_ref.shape[0], 256, sums.shape[1]
    places = [lax.rem(place_ref[0] + shift + n, n) for shift in shifts]
    fetch = tile_fetch(places, whole_hbm, whole, sems, tile)
    full, rest = width // tile, width % tile
    last = (full, full * tile, rest)

    def part(j):
        return j, pl.multiple_of(j * tile, tile), tile

    def operands(j, start, size):
        copies = fetch(j, start, size)
        if follows:
            columns = pl.ds(start, size)
            place = sems.at[(count + 1) * (full + 1) + j]
            copies.append(pltpu.make_async_copy(before[0].at[:, columns], sums.at[:, columns], place))
        return copies

    @pl.loop(0, full)
    def _(j):
        run(operands(*part(j)), "start")

    run(operands(*last), "start")
    squares = before[1][...] if follows else jnp.zeros((blocks[0].shape[0], 1), F32)
    squares_ref[...] = scaled_blocks(blocks, [gain_ref[at] for at in places], scaled, squares)

    def result(j, start, size):
        columns = pl.ds(start, size)
        place = sems.at[count * (full + 1) + j]
        return pltpu.make_async_copy(sums.at[:, columns], sums_hbm.at[:, columns], place)

    def step(j, start, size):
        run(operands(j, start, size), "wait")
        columns = pl.ds(start, size)
        total = jnp.dot(scaled[...], whole[:, columns], preferred_element_type=F32)
        sums[:, columns] = sums[:, columns] + total if follows else total
        result(j, start, size).start()

    @pl.loop(0, full)
    def _(j):
        step(*part(j))

    step(*last)

    @pl.loop(0, full)
    def _(j):
        result(*part(j)).wait()

    result(*last).wait()


def late_kernel(shifts, early, units, place_ref, *refs):
    n = len(shifts)
    blocks, gain_ref, whole_hbm, sums_hbm, squares_ref, hidden_ref, own_ref = refs[:n], *refs[n : n + 6]
    scaled, whole, sums, sems = refs[n + 6 :]
    tile = 256
    places = [lax.rem(place_ref[0] + shift + n, n) for shift in shifts]
    fetch = tile_fetch(places[early:], whole_hbm, whole, sems, tile)
    width = whole.shape[1]
    tiles = pl.cdiv(width, tile)
    apart = width - units
    full, rest = units // tile, units % tile

    def both(j, start, size):
        copies = []
        whole_tiles = size if size == tile else apart - full * tile
        for k, first, size in ((0, 0, whole_tiles), (full + 1, apart, size)):
            copies += fetch(k + j, first + start, size)
            columns = pl.ds(first + start, size)
            place = sems.at[(n - early) * tiles + k + j]
            copies.append(pltpu.make_async_copy(sums_hbm.at[:, columns], sums.at[:, columns], place))
        return copies

    last = (full, full * tile, rest)

    def part(j):
        return j, pl.multiple_of(j * tile, tile), tile

    @pl.loop(0, full)
    def _(j):
        run(both(*part(j)), "start")

    run(both(*last), "start")
    gains = [gain_ref[at] for at in places[early:]]
    squares = scaled_blocks(blocks[early:], gains, scaled, squares_ref[...])
    scale = lax.rsqrt(squares / whole_hbm.shape[0] + EPSILON)
    own = own_ref.shape[1]
    first = pl.multiple_of(place_ref[0] * own, own)
    for at, block in zip(places, blocks):
        own_ref[at] = block[pl.ds(first, own), :]

    def step(j, start, size):
        run(both(j, start, size), "wait")
        gate, upward = (
            scale
            * (
                sums[:, pl.ds(at, size)]
                + jnp.dot(scaled[...], whole[:, pl.ds(at, size)], preferred_element_type=F32)
            )
            for at in (start, apart + start)
        )
        value = gate * (1.0 / (1.0 + jnp.exp(-gate))) * upward
        hidden_ref[:, pl.ds(start, size)] = value.astype(BF16)

    @pl.loop(0, full)
    def _(j):
        step(*part(j))

    step(*last)


def down_kernel(tile, hidden_ref, weight_hbm, out_hbm, weight, out, sems):
    tiles = weight.shape[0] // tile

    def here(j):
        return pl.ds(pl.multiple_of(j * tile, tile), tile)

    def part(j):
        return pltpu.make_async_copy(weight_hbm.at[here(j), :], weight.at[here(j), :], sems.at[j])

    def result(j):
        return pltpu.make_async_copy(out.at[:, here(j)], out_hbm.at[:, here(j)], sems.at[tiles + j])

    @pl.loop(0, tiles)
    def _(j):
        part(j).start()

    @pl.loop(0, tiles)
    def _(j):
        part(j).wait()
        out[:, here(j)] = turned_dot(hidden_ref[...], weight[here(j), :]).astype(BF16)
        result(j).start()

    @pl.loop(0, tiles)
    def _(j):
        result(j).wait()


def call(kernel, out_shape, specs, flops, scratch=(), mib=16, out_space=VMEM):
    def run(*args):
        moved = sum(a.size * a.dtype.itemsize for a in args)
        if isinstance(out_shape, tuple):
            spaces = out_space if isinstance(out_space, tuple) else (out_space,) * len(out_shape)
            outs = tuple(pl.BlockSpec(memory_space=space) for space in spaces)
        else:
            outs = pl.BlockSpec(memory_space=out_space)
        return pl.pallas_call(
            kernel,
            out_shape=out_shape,
            in_specs=specs,
            out_specs=outs,
            scratch_shapes=scratch,
            compiler_params=pltpu.CompilerParams(vmem_limit_bytes=mib << 20),
            cost_estimate=pl.CostEstimate(flops=flops, bytes_accessed=moved, transcendentals=0),
        )(*args)

    return run


def body(
    patches,
    window_ids,
    vit_gain,
    qkv_weight,
    out_weight,
    merge_gain,
    merger_weight,
    audio,
    span_lengths,
    span_time,
    llm_gain,
    gate_weight,
    up_weight,
    down_weight,
):
    patch_count, d_vit = patches.shape
    n = lax.axis_size("tensor")
    owner_count = lax.axis_size("dp")
    owner = lax.axis_index("dp")
    plane = lax.axis_index("tensor")
    core = lax.rem(owner, 2)
    units = gate_weight.shape[1]
    vmem = pl.BlockSpec(memory_space=VMEM)
    smem = pl.BlockSpec(memory_space=SMEM)
    hbm = pl.BlockSpec(memory_space=HBM)

    windows = window_ids[0]
    context = call(
        vision_kernel,
        jax.ShapeDtypeStruct((2 * HEAD_VIT, patch_count), BF16),
        [smem] + [vmem] * 5,
        2 * patch_count * (3 * d_vit * 160 + 4 * patch_count * HEAD_VIT),
    )(
        core.reshape(1),
        patches,
        windows[:, None],
        windows[None, :],
        vit_gain[None, :],
        jnp.swapaxes(qkv_weight, 1, 2),
    )

    video_rows = patch_count // 4
    seq_count = video_rows + audio.shape[0]
    capacity = 2 * seq_count // owner_count
    sent_lengths = span_lengths[owner]
    starts = jnp.cumsum(sent_lengths) - sent_lengths
    slot_index = jnp.arange(capacity, dtype=jnp.int32)
    row_of_slot = jnp.where(
        slot_index[None, :] < sent_lengths[:, None], starts[:, None] + slot_index[None, :], -1
    ).reshape(-1)
    row = jnp.arange(seq_count, dtype=jnp.int32)
    select = (row_of_slot[:, None] == row[None, video_rows:]).astype(BF16)
    from_audio = jnp.dot(select, audio, preferred_element_type=F32).astype(BF16)
    group = 2 * HEAD_VIT
    own_head = lax.dynamic_slice_in_dim(out_weight, core * HEAD_VIT, HEAD_VIT, 0)
    above = lax.ppermute(own_head, "tensor", shifted("tensor", 1))
    below = lax.ppermute(own_head, "tensor", shifted("tensor", -1))
    split, block_rows = group * patch_count // 128, HEAD_VIT * d_vit // 128
    payload = jax.ShapeDtypeStruct((split + block_rows, 128), BF16)
    up, down = call(pack_kernel, (payload, payload), [vmem] * 3, 0)(context, above, below)
    ups, downs = [up], [down]
    for k in range(1, n // 2):
        if k == 2:
            ups[-1], from_audio, slot_column = lax.optimization_barrier(
                (ups[-1], from_audio, row_of_slot[:, None])
            )
        ups.append(lax.ppermute(ups[-1], "tensor", shifted("tensor", 1)))
        downs.append(lax.ppermute(downs[-1], "tensor", shifted("tensor", -1)))
    ups.append(lax.ppermute(ups[-1][:split], "tensor", shifted("tensor", 1)))
    contexts = [up]
    tall = []
    for k in range(1, n // 2 + 1):
        contexts.append(ups[k])
        if k < n // 2:
            contexts.append(downs[k])
            tall.append(ups[k])
        if k < n // 2 - 1:
            tall.append(downs[k])
    swap = [(i, i ^ 1) for i in range(owner_count)]
    laid = call(
        functools.partial(stack_kernel, 3),
        jax.ShapeDtypeStruct((n - 1, block_rows, 128), BF16),
        [vmem] * (n - 1),
        0,
    )(own_head, above, below, *tall[:-1])
    other = lax.ppermute(laid, "dp", swap)
    last = lax.ppermute(tall[-1], "dp", swap)

    gap = -units % 128
    stacked = jnp.concatenate(
        [gate_weight, jnp.zeros((gate_weight.shape[0], gap), BF16), up_weight], axis=1
    )
    whole = lax.all_gather(stacked, "dp", axis=0, tiled=True)

    slots = owner_count * capacity
    width = audio.shape[1]
    operands = [*contexts[: n - 1], own_head, above, below, other, patches]
    sofar = call(
        functools.partial(project_kernel, n),
        jax.ShapeDtypeStruct((patch_count, d_vit), F32),
        [hbm] * len(operands),
        2 * patch_count * d_vit * d_vit,
        scratch=[pltpu.VMEM(a.shape, BF16) for a in operands]
        + [
            pltpu.VMEM(((n - 1) * group, patch_count), BF16),
            pltpu.VMEM(((n - 1) * group, d_vit), BF16),
            pltpu.SemaphoreType.DMA((len(operands),)),
        ],
        mib=62,
    )(*operands)
    outgoing = call(
        merge_kernel,
        jax.ShapeDtypeStruct((slots, width), BF16),
        [vmem] * 5 + [hbm, vmem, hbm],
        2 * patch_count * d_vit * width,
        scratch=[
            pltpu.VMEM((group, patch_count), BF16),
            pltpu.VMEM((group, d_vit), BF16),
            pltpu.VMEM((d_vit // 128, patch_count, 128), F32),
            pltpu.VMEM(merger_weight.shape[::-1], BF16),
            pltpu.VMEM((slots, width), BF16),
            pltpu.SemaphoreType.DMA((2,)),
        ],
        mib=62,
    )(
        contexts[n - 1],
        tall[-1],
        last,
        sofar,
        merge_gain[None, :],
        merger_weight.T,
        slot_column,
        from_audio,
    )
    down_turned, outgoing = lax.optimization_barrier((down_weight.T, outgoing))
    down_whole = lax.all_gather(down_turned, "dp", axis=0, tiled=True)
    incoming = lax.all_to_all(
        outgoing.reshape(owner_count, capacity, width), "dp", split_axis=0, concat_axis=0, tiled=True
    ).reshape(slots, width)
    taken_lengths = span_lengths[:, owner]
    arrival = span_time[owner]
    earlier = arrival[:, None] < arrival[None, :]
    offsets = jnp.sum(jnp.where(earlier, taken_lengths[:, None], 0), axis=0)
    target = jnp.where(
        slot_index[None, :] < taken_lengths[:, None], offsets[:, None] + slot_index[None, :], -1
    ).reshape(1, -1)
    sequence = call(
        pick_kernel,
        jax.ShapeDtypeStruct((seq_count, width), BF16),
        [vmem] * 2,
        2 * slots * seq_count * width,
        mib=16,
    )(target, incoming)

    features = n * width
    own_count = seq_count // n
    shifts = [0]
    for k in range(1, n // 2):
        shifts += [-k, k]
    shifts.append(-(n // 2))
    stages = ((0, 5), (5, 7))
    early = stages[-1][1]
    here = plane.reshape(1)
    padded = 2 * units + gap
    gains = llm_gain.reshape(n, 1, width)
    tiles = pl.cdiv(padded, 256)

    def scratch(count):
        return [
            pltpu.VMEM((seq_count, count * width), BF16),
            pltpu.VMEM((count * width, padded), BF16),
            pltpu.VMEM((seq_count, padded), F32),
            pltpu.SemaphoreType.DMA(((count + 2) * tiles,)),
        ]

    def products(first, last, blocks, before):
        return call(
            functools.partial(early_kernel, shifts[first:last], len(before) // 2),
            (
                jax.ShapeDtypeStruct((seq_count, padded), F32),
                jax.ShapeDtypeStruct((seq_count, 1), F32),
            ),
            [smem] + [vmem] * (last - first + 1) + [hbm] + [hbm, vmem][: len(before)],
            4 * seq_count * (last - first) * width * units,
            scratch=scratch(last - first),
            mib=48,
            out_space=(HBM, VMEM),
        )(here, *blocks[first:last], gains, whole, *before)

    blocks = [sequence]
    sums = ()
    a = b = sequence
    for k in range(1, n // 2 + 1):
        a = lax.ppermute(a, "tensor", shifted("tensor", 1))
        if k < n // 2:
            b = lax.ppermute(b, "tensor", shifted("tensor", -1))
        if k >= n // 2 - 1:
            sums = products(*stages[k - n // 2 + 1], blocks, tuple(sums))
            a, b, sums = lax.optimization_barrier((a, b, sums))
        blocks.append(a)
        if k < n // 2:
            blocks.append(b)
    hidden, own_rows = call(
        functools.partial(late_kernel, shifts, early, units),
        (
            jax.ShapeDtypeStruct((seq_count, units), BF16),
            jax.ShapeDtypeStruct((n, own_count, width), BF16),
        ),
        [smem] + [vmem] * (n + 1) + [hbm] * 2 + [vmem],
        4 * seq_count * (n - early) * width * units,
        scratch=scratch(n - early),
        mib=48,
    )(here, *blocks, gains, whole, *sums)
    down_tile = 512
    terms = call(
        functools.partial(down_kernel, down_tile),
        jax.ShapeDtypeStruct((seq_count, features), BF16),
        [vmem, hbm],
        2 * seq_count * features * units,
        scratch=[
            pltpu.VMEM((features, units), BF16),
            pltpu.VMEM((seq_count, features), BF16),
            pltpu.SemaphoreType.DMA((2 * (features // down_tile),)),
        ],
        mib=62,
        out_space=HBM,
    )(hidden, down_whole)
    summed = lax.psum_scatter(terms, "tensor", scatter_dimension=0, tiled=True).astype(F32)
    own_rows = jnp.moveaxis(own_rows, 0, 1).reshape(own_count, features)
    return (own_rows.astype(F32) + summed).astype(BF16)


def solution(mesh):
    return jax.shard_map(
        body,
        mesh=mesh,
        in_specs=(
            P("dp", None),
            P("dp", None),
            P(),
            P(None, None, "tensor"),
            P("tensor", None),
            P(),
            P(None, "tensor"),
            P("dp", "tensor"),
            P(),
            P(),
            P(),
            P("dp", "tensor"),
            P("dp", "tensor"),
            P("tensor", "dp"),
        ),
        out_specs=P(("dp", "tensor"), None),
        check_vma=False,
    )
```
